32 devices in a mesh: group: 1, ctx: 32 (over z, y, x, core).
Axes of the slice: x: 2, y: 2, z: 4, core: 2. Of those that a mesh axis runs over, the one named last changes fastest.
Arguments:
- history: bfloat16 [2, 1024, 8192], P('group', 'ctx'), may hold values from -6 to 6
- lengths: int32 [2], P('group'), may hold values from 256 to 1024
- token_ids: int32 [2, 512], P('group'), may hold values from 0 to 511
- embed: bfloat16 [512, 8192], P('ctx'), may hold values from -6 to 6
- residue: float32 [16, 8192], replicated, may hold values from -0.046875 to 0.046875
- decay: float32 [16, 8192], replicated, may hold values from 0.1 to 400
- skip: float32 [8192], replicated, may hold values from 0.5 to 1.5
Outputs:
- mixed: bfloat16 [2, 512, 8192], P('group', 'ctx')
The draws below stay inside these ranges and needn't reach their ends.
Inputs may be any that keep to these rules, and one draw needn't show every extreme that they name: `lengths`: history positions at or past a sequence's length are ignored.
All inputs are finite; a program needn't handle non-finite values.
Results may differ from the reference program's by a relative error of at most 0.0005.
Values may be sent and summed in bfloat16 or wider, within the bound.
No kernel may reach another device: no remote copies, remote signals or barrier semaphores. Data moves between devices by JAX's collectives and lax.ppermute only.
A program may use at most 128 MiB of HBM per device.

```python
import math
import jax
import jax.numpy as jnp
from jax import lax

D = 8192
VOCAB = 512
MODES = 16
SEQS = 2
L_DEV = 32
STEP_LEN = 128
STEPS = 4
GEN = 512
CTX = 1024


def touch_ends(array, own_key, low, largest):
    extent = array.shape
    place = [jax.random.randint(jax.random.fold_in(own_key, axis), (), 0, extent[axis]) for axis in range(len(extent))]
    array = array.at[tuple(place)].set(low)
    longest = extent.index(max(extent))
    place[longest] = (place[longest] + 1) % extent[longest]
    return array.at[tuple(place)].set(largest)


def shard_levels(stream_key, dims, split, low, high):
    level, own = 1.0, jax.random.fold_in(stream_key, 6)
    for dim, shards_of in split:
        heights = jnp.exp(jax.random.uniform(jax.random.fold_in(own, dim), (shards_of,), jnp.float32, low / len(split), high / len(split)))
        level = level * jnp.repeat(heights, dims[dim] // shards_of).reshape([-1 if axis == dim else 1 for axis in range(len(dims))])
    return level


def noise(key, dims, deviation, most, split=(), kind=jnp.bfloat16):
    drawn = jax.random.normal(key, dims, jnp.float32) * deviation
    if len(split) > 0:
        drawn = shard_levels(key, dims, split, -0.22, 0.18) * drawn
    return jnp.clip(drawn, min=-most, max=most).astype(kind)


def setup_inputs(seed: int = 0, part: int = 0) -> dict:
    arg_keys = jax.random.split(jax.random.key(seed), 8)
    part_splits = jax.random.split(jax.random.fold_in(arg_keys[7], part), 8)
    history = noise(part_splits[0], (SEQS, CTX, D), 1.0, 6.0, ((1, 32),))
    lengths = jax.random.randint(part_splits[1], (SEQS,), CTX // 4, CTX + 1).astype(jnp.int32)
    token_ids = touch_ends(jax.random.randint(part_splits[2], (SEQS, GEN), 0, VOCAB), jax.random.fold_in(part_splits[2], 1), 0, VOCAB - 1).astype(jnp.int32)
    embed = noise(arg_keys[3], (VOCAB, D), 1.0, 6.0, ((0, 32),))
    residue = noise(arg_keys[4], (MODES, D), (MODES * CTX) ** -0.5, 0.046875, (), jnp.float32)
    decay = jnp.clip(jnp.exp(jax.random.uniform(arg_keys[5], (MODES, D), jnp.float32, math.log(0.1), math.log(400.0))), 0.1, 400.0)
    skip = jnp.clip(jax.random.uniform(arg_keys[6], (D,), jnp.float32, 0.5, 1.5), 0.5, 1.5)
    return {"history": history, "lengths": lengths, "token_ids": token_ids, "embed": embed, "residue": residue, "decay": decay, "skip": skip}


def reference(history, lengths, token_ids, embed, residue, decay, skip):
    seqs = history.shape[0]
    width = history.shape[2]
    rate = decay / CTX
    blocks = CTX // L_DEV

    def block_state(carry, index):
        start = index * L_DEV
        piece = lax.dynamic_slice_in_dim(history, start, L_DEV, 1)
        places = start + jnp.arange(L_DEV, dtype=jnp.int32)
        inside = places[None, :] < lengths[:, None]
        masked = jnp.where(inside[:, :, None], piece, jnp.zeros_like(piece)).astype(jnp.float32)
        ends = start + L_DEV
        lift = jnp.maximum(lengths - ends, -L_DEV).astype(jnp.float32)
        local = jnp.exp(-rate[:, None, :] * (ends - places).astype(jnp.float32)[None, :, None])
        part = jnp.einsum("ksc,bsc->kbc", local, masked, precision=lax.Precision.HIGHEST)
        return carry + part * jnp.exp(-rate[:, None, :] * lift[None, :, None]), None

    state, _ = lax.scan(block_state, jnp.zeros((MODES, seqs, width), jnp.float32), jnp.arange(blocks, dtype=jnp.int32))
    fresh = embed[token_ids]
    times = jnp.arange(GEN, dtype=jnp.int32).astype(jnp.float32)
    decays = jnp.exp(-rate[:, None, :] * times[None, :, None])
    weighted = residue[:, None, :] * decays
    kernel = jnp.sum(weighted, axis=0)
    history_part = jnp.einsum("ktc,kbc->btc", weighted, state, precision=lax.Precision.HIGHEST)
    pieces = fresh.astype(jnp.float32).reshape(seqs, STEPS, STEP_LEN, width)
    ladder = jnp.arange(STEP_LEN, dtype=jnp.int32)
    totals = [jnp.zeros((seqs, STEP_LEN, width), jnp.float32) for _ in range(STEPS)]
    for delta in range(STEPS):
        offset = delta * STEP_LEN + ladder[:, None] - ladder[None, :]
        toeplitz = jnp.where((offset >= 0)[:, :, None], jnp.take(kernel, jnp.maximum(offset, 0), axis=0), 0.0)
        for later in range(delta, STEPS):
            totals[later] = totals[later] + jnp.einsum("tsc,bsc->btc", toeplitz, pieces[:, later - delta], precision=lax.Precision.HIGHEST)
    conv_part = jnp.concatenate(totals, axis=1)
    mixed = history_part + conv_part + skip[None, None, :] * fresh.astype(jnp.float32)
    return mixed.astype(jnp.bfloat16)
```

```python
import jax
import jax.numpy as jnp
from jax import lax
from jax.experimental import pallas as pl
from jax.experimental.pallas import tpu as pltpu
from jax.sharding import PartitionSpec as P

ROWS = 8


def lanes_of(block):
    return 256 if block % 256 == 0 else block


def lost(rate):
    series = jnp.ones_like(rate)
    for k in range(12, 1, -1):
        series = 1.0 - rate * series * (1.0 / k)
    return jnp.where(rate < 0.5, rate * series, 1.0 - jnp.exp(-rate))


def merge_rows(parts):
    shape = parts[0].shape
    row = lax.broadcasted_iota(jnp.int32, shape, 0)
    low = row < 4
    level = [
        jnp.where(low, parts[i], parts[i + 4]) + pltpu.roll(jnp.where(low, parts[i + 4], parts[i]), 4, 0)
        for i in range(4)
    ]
    for gap in (2, 1):
        first = (row & gap) == 0
        level = [
            jnp.where(first, level[i], level[i + gap])
            + jnp.where(first, pltpu.roll(level[i], 8 - gap, 0), pltpu.roll(level[i + gap], gap, 0))
            for i in range(gap)
        ]
    return level[0]


def fold(x):
    total = x[:ROWS]
    for start in range(ROWS, x.shape[0], ROWS):
        total = total + x[start : start + ROWS]
    return total


def history_kernel(total_len, where_ref, lengths_ref, own_ref, other_ref, decay_ref, out_ref, wide):
    seqs, tile, block = own_ref.shape
    me = where_ref[0]
    partner = me + 1 - 2 * lax.rem(me, 2)
    row = lax.broadcasted_iota(jnp.int32, (tile, block), 0)
    for side, (ref, owner) in enumerate(((own_ref, me), (other_ref, partner))):
        for b in range(seqs):
            left = lengths_ref[b] - owner * tile
            wide[side, b] = jnp.where(row < left, ref[b].astype(jnp.float32), 0.0)
    lanes = lanes_of(block)
    for start in range(0, block, lanes):
        at = slice(start, start + lanes)
        rate = decay_ref[:, at] / total_len
        keep = jnp.exp(-rate)
        chains = [(side, b) for side in range(2) for b in range(seqs)]

        def step(s, sums):
            return tuple(
                keep * total + wide[side, b, pl.ds(s, 1), at] for (side, b), total in zip(chains, sums)
            )

        zero = jnp.zeros(rate.shape, jnp.float32)
        sums = lax.fori_loop(0, tile, step, (zero,) * len(chains), unroll=8)
        for b in range(seqs):
            total = zero
            for side, owner in enumerate((me, partner)):
                after = jnp.maximum(lengths_ref[b] - (owner + 1) * tile, -tile) + 1
                total = total + sums[side * seqs + b] * jnp.exp(-rate * after.astype(jnp.float32))
            out_ref[0, b, :, at] = total


def fresh_kernel(total_len, where_ref, tokens_ref, table_ref, decay_ref, residue_ref, skip_ref, out_ref, fresh):
    seqs, gen = tokens_ref.shape
    span = out_ref.shape[1]
    vocab, lanes = table_ref.shape
    table = table_ref[...]
    entry = lax.broadcasted_iota(jnp.int32, (vocab, gen), 0)
    for b in range(seqs):
        chosen = jnp.where(entry == tokens_ref[b : b + 1, :], 1.0, 0.0).astype(jnp.bfloat16)
        fresh[b] = lax.dot_general(
            chosen, table, (((0,), (0,)), ((), ())), preferred_element_type=jnp.float32
        )
    rate = decay_ref[...] / total_len
    gone = lost(rate)
    residue = residue_ref[...]
    skip = skip_ref[...]
    skipped = where_ref[1] * span

    def advance(total, b, t):
        return (total + fresh[b, pl.ds(t, 1), :]) - total * gone

    def before(index, sums):
        sums = list(sums)
        for j in range(ROWS):
            sums = [advance(sums[b], b, index * ROWS + j) for b in range(seqs)]
        return tuple(sums)

    def after(index, sums):
        sums = list(sums)
        parts = [[] for _ in range(seqs)]
        first = pl.multiple_of(skipped + index * ROWS, ROWS)
        for j in range(ROWS):
            for b in range(seqs):
                sums[b] = advance(sums[b], b, first + j)
                parts[b].append(fold(residue * sums[b]))
        for b in range(seqs):
            rows = pl.ds(pl.multiple_of(index * ROWS, ROWS), ROWS)
            out_ref[b, rows, :] = merge_rows(parts[b]) + skip * fresh[b, pl.ds(first, ROWS), :]
        return tuple(sums)

    zero = jnp.zeros(rate.shape, jnp.float32)
    sums = lax.fori_loop(0, lax.div(skipped, ROWS), before, (zero,) * seqs)
    lax.fori_loop(0, span // ROWS, after, sums)


def mix_kernel(total_len, where_ref, near_ref, far_ref, fresh_ref, decay_ref, residue_ref, out_ref):
    seqs, span, lanes = fresh_ref.shape
    rate = decay_ref[...] / total_len
    keep = jnp.exp(-rate)
    states = [residue_ref[...] * (near_ref[b] + far_ref[b]) for b in range(seqs)]
    skipped = where_ref[1] * span
    chunk = 2 * ROWS

    def step(index, _):
        first = pl.multiple_of(index * chunk, chunk)
        scale = jnp.exp(-rate * (skipped + first).astype(jnp.float32))
        terms = [states[b] * scale for b in range(seqs)]
        done = [[] for _ in range(seqs)]
        for _ in range(chunk // ROWS):
            parts = [[] for _ in range(seqs)]
            for _ in range(ROWS):
                for b in range(seqs):
                    parts[b].append(fold(terms[b]))
                    terms[b] = terms[b] * keep
            for b in range(seqs):
                done[b].append(merge_rows(parts[b]))
        for b in range(seqs):
            mixed = jnp.concatenate(done[b], axis=0) + fresh_ref[b, pl.ds(first, chunk), :]
            if len(out_ref.shape) == 4:
                own = out_ref.shape[2]
                spot = pl.ds(pl.multiple_of(lax.rem(first, own), chunk), chunk)
                out_ref[lax.div(first, own), b, spot, :] = mixed.astype(jnp.bfloat16)
            else:
                out_ref[b, pl.ds(first, chunk), :] = mixed.astype(jnp.bfloat16)
        return 0

    lax.fori_loop(0, span // chunk, step, 0)


def body(history, lengths, token_ids, embed, residue, decay, skip):
    devices = lax.axis_size("ctx")
    me = lax.axis_index("ctx")
    seqs, tile, width = history.shape
    modes = decay.shape[0]
    gen = token_ids.shape[1]
    total_len = float(tile * devices)
    team = devices // 2
    chips = team // 2
    block = width // team
    lanes = lanes_of(block)
    pieces = block // lanes
    span = gen // 2
    own = gen // devices
    half = me // team
    mine = lax.rem(me, 2) * chips + lax.rem(me, team) // 2
    where = jnp.stack([me, half, mine]).astype(jnp.int32)
    f32 = jnp.float32

    swapped = lax.ppermute(history, "ctx", [(j, j ^ 1) for j in range(devices)])

    rows = embed.shape[0]
    columns = embed.reshape(rows, 2, chips, block).transpose(2, 1, 0, 3).reshape(team, rows, block)
    table = lax.all_to_all(jnp.concatenate([columns, columns]), "ctx", 0, 0, tiled=True)
    table = table.reshape(devices * rows, block)

    part = lambda g, at, ln: (0, 0, lax.rem(at[0], 2) * chips + g)
    partial = pl.pallas_call(
        lambda *refs: history_kernel(total_len, *refs),
        grid_spec=pltpu.PrefetchScalarGridSpec(
            num_scalar_prefetch=2,
            grid=(chips,),
            in_specs=[
                pl.BlockSpec((seqs, tile, block), part),
                pl.BlockSpec((seqs, tile, block), part),
                pl.BlockSpec((modes, block), lambda g, at, ln: part(g, at, ln)[1:]),
            ],
            out_specs=pl.BlockSpec((1, seqs, modes, block), lambda g, at, ln: (g, 0, 0, 0)),
            scratch_shapes=[pltpu.VMEM((2, seqs, tile, block), f32)],
        ),
        out_shape=jax.ShapeDtypeStruct((chips, seqs, modes, block), f32),
        cost_estimate=pl.CostEstimate(
            flops=4 * seqs * tile * modes * block * chips, bytes_accessed=3 * 2**20, transcendentals=0
        ),
        name="history_states",
    )(where, lengths, history, swapped, decay)
    sides = [[h * team + 2 * q + c for q in range(chips)] for h in range(2) for c in range(2)]
    gathered = lax.all_to_all(partial, "ctx", 0, 0, tiled=True, axis_index_groups=sides)
    near = jnp.sum(gathered, axis=0)
    far = lax.ppermute(near, "ctx", [(j, (j + team) % devices) for j in range(devices)])

    strip = lambda g, at: (0, at[2] * pieces + g)
    fresh = pl.pallas_call(
        lambda *refs: fresh_kernel(total_len, *refs),
        grid_spec=pltpu.PrefetchScalarGridSpec(
            num_scalar_prefetch=1,
            grid=(pieces,),
            in_specs=[
                pl.BlockSpec((seqs, gen), lambda g, at: (0, 0)),
                pl.BlockSpec((devices * rows, lanes), lambda g, at: (0, g)),
                pl.BlockSpec((modes, lanes), strip),
                pl.BlockSpec((modes, lanes), strip),
                pl.BlockSpec((1, lanes), strip),
            ],
            out_specs=pl.BlockSpec((seqs, span, lanes), lambda g, at: (0, 0, g)),
            scratch_shapes=[pltpu.VMEM((seqs, gen, lanes), f32)],
        ),
        out_shape=jax.ShapeDtypeStruct((seqs, span, block), f32),
        cost_estimate=pl.CostEstimate(
            flops=6 * seqs * span * modes * block, bytes_accessed=2**21, transcendentals=0
        ),
        name="fresh_scan",
    )(where, token_ids, table, decay, residue, skip.reshape(1, width))

    direct = own % (2 * ROWS) == 0
    state = pl.BlockSpec((seqs, modes, lanes), lambda g, at: (0, 0, g))
    if direct:
        out_shape = (team, seqs, own, block)
        out_spec = pl.BlockSpec((team, seqs, own, lanes), lambda g, at: (0, 0, 0, g))
    else:
        out_shape = (seqs, span, block)
        out_spec = pl.BlockSpec((seqs, span, lanes), lambda g, at: (0, 0, g))
    mixed = pl.pallas_call(
        lambda *refs: mix_kernel(total_len, *refs),
        grid_spec=pltpu.PrefetchScalarGridSpec(
            num_scalar_prefetch=1,
            grid=(pieces,),
            in_specs=[
                state,
                state,
                pl.BlockSpec((seqs, span, lanes), lambda g, at: (0, 0, g)),
                pl.BlockSpec((modes, lanes), strip),
                pl.BlockSpec((modes, lanes), strip),
            ],
            out_specs=out_spec,
        ),
        out_shape=jax.ShapeDtypeStruct(out_shape, jnp.bfloat16),
        cost_estimate=pl.CostEstimate(
            flops=3 * seqs * span * modes * block, bytes_accessed=2**21, transcendentals=0
        ),
        name="mix_states",
    )(where, near, far, fresh, decay, residue)
    if not direct:
        mixed = mixed.reshape(seqs, team, own, block).transpose(1, 0, 2, 3)
    halves = [[h * team + p for p in range(team)] for h in range(2)]
    result = lax.all_to_all(mixed, "ctx", 0, 0, tiled=True, axis_index_groups=halves)
    result = result.reshape(chips, 2, seqs, own, block).transpose(2, 3, 1, 0, 4)
    return result.reshape(seqs, own, width)


def solution(mesh):
    placed = (P("group", "ctx", None), P("group"), P("group", None), P("ctx", None), P(), P(), P())
    return jax.shard_map(
        body, mesh=mesh, in_specs=placed, out_specs=P("group", "ctx", None), check_vma=False
    )
```

```python
import jax
import jax.numpy as jnp
from jax import lax
from jax.experimental import pallas as pl
from jax.experimental.pallas import tpu as pltpu
from jax.sharding import PartitionSpec as P

ROWS = 8


def lanes_of(block):
    return 256 if block % 256 == 0 else block


def lost(rate):
    series = jnp.ones_like(rate)
    for k in range(12, 1, -1):
        series = 1.0 - rate * series * (1.0 / k)
    return jnp.where(rate < 0.5, rate * series, 1.0 - jnp.exp(-rate))


def merge_rows(parts):
    shape = parts[0].shape
    row = lax.broadcasted_iota(jnp.int32, shape, 0)
    low = row < 4
    level = [
        jnp.where(low, parts[i], parts[i + 4]) + pltpu.roll(jnp.where(low, parts[i + 4], parts[i]), 4, 0)
        for i in range(4)
    ]
    for gap in (2, 1):
        first = (row & gap) == 0
        level = [
            jnp.where(first, level[i], level[i + gap])
            + jnp.where(first, pltpu.roll(level[i], 8 - gap, 0), pltpu.roll(level[i + gap], gap, 0))
            for i in range(gap)
        ]
    return level[0]


def fold(x):
    total = x[:ROWS]
    for start in range(ROWS, x.shape[0], ROWS):
        total = total + x[start : start + ROWS]
    return total


def history_kernel(total_len, where_ref, lengths_ref, own_ref, other_ref, decay_ref, out_ref, wide):
    seqs, tile, block = own_ref.shape
    me = where_ref[0]
    partner = me + 1 - 2 * lax.rem(me, 2)
    row = lax.broadcasted_iota(jnp.int32, (tile, block), 0)
    for side, (ref, owner) in enumerate(((own_ref, me), (other_ref, partner))):
        for b in range(seqs):
            left = lengths_ref[b] - owner * tile
            wide[side, b] = jnp.where(row < left, ref[b].astype(jnp.float32), 0.0)
    lanes = lanes_of(block)
    for start in range(0, block, lanes):
        at = slice(start, start + lanes)
        rate = decay_ref[:, at] / total_len
        keep = jnp.exp(-rate)
        chains = [(side, b) for side in range(2) for b in range(seqs)]

        def step(s, sums):
            return tuple(
                keep * total + wide[side, b, pl.ds(s, 1), at] for (side, b), total in zip(chains, sums)
            )

        zero = jnp.zeros(rate.shape, jnp.float32)
        sums = lax.fori_loop(0, tile, step, (zero,) * len(chains), unroll=8)
        for b in range(seqs):
            total = zero
            for side, owner in enumerate((me, partner)):
                after = jnp.maximum(lengths_ref[b] - (owner + 1) * tile, -tile) + 1
                total = total + sums[side * seqs + b] * jnp.exp(-rate * after.astype(jnp.float32))
            out_ref[0, b, :, at] = total


def fresh_kernel(total_len, where_ref, tokens_ref, table_ref, far_ref, decay_ref, residue_ref, skip_ref, out_ref, fresh):
    seqs, gen = tokens_ref.shape
    span = out_ref.shape[1]
    vocab = table_ref.shape[0]
    entry = lax.broadcasted_iota(jnp.int32, (vocab, gen), 0)
    for b in range(seqs):
        found = 0.0
        for ref, side in ((table_ref, where_ref[1]), (far_ref, 1 - where_ref[1])):
            chosen = jnp.where(entry == tokens_ref[b : b + 1, :] - side * vocab, 1.0, 0.0).astype(jnp.bfloat16)
            found = found + lax.dot_general(
                chosen, ref[...], (((0,), (0,)), ((), ())), preferred_element_type=jnp.float32
            )
        fresh[b] = found
    rate = decay_ref[...] / total_len
    gone = lost(rate)
    residue = residue_ref[...]
    skip = skip_ref[...]
    skipped = where_ref[1] * span

    def advance(total, b, t):
        return (total + fresh[b, pl.ds(t, 1), :]) - total * gone

    def before(index, sums):
        sums = list(sums)
        for j in range(ROWS):
            sums = [advance(sums[b], b, index * ROWS + j) for b in range(seqs)]
        return tuple(sums)

    def after(index, sums):
        sums = list(sums)
        parts = [[] for _ in range(seqs)]
        first = pl.multiple_of(skipped + index * ROWS, ROWS)
        for j in range(ROWS):
            for b in range(seqs):
                sums[b] = advance(sums[b], b, first + j)
                parts[b].append(fold(residue * sums[b]))
        for b in range(seqs):
            rows = pl.ds(pl.multiple_of(index * ROWS, ROWS), ROWS)
            out_ref[b, rows, :] = merge_rows(parts[b]) + skip * fresh[b, pl.ds(first, ROWS), :]
        return tuple(sums)

    zero = jnp.zeros(rate.shape, jnp.float32)
    sums = lax.fori_loop(0, lax.div(skipped, ROWS), before, (zero,) * seqs)
    lax.fori_loop(0, span // ROWS, after, sums)


def mix_kernel(total_len, where_ref, near_ref, far_ref, fresh_ref, decay_ref, residue_ref, out_ref):
    seqs, span, _ = fresh_ref.shape
    rate = decay_ref[...] / total_len
    keep = jnp.exp(-rate)
    states = [residue_ref[...] * (near_ref[b] + far_ref[b]) for b in range(seqs)]
    skipped = where_ref[1] * span
    chunk = 2 * ROWS

    def step(index, _):
        first = pl.multiple_of(index * chunk, chunk)
        scale = jnp.exp(-rate * (skipped + first).astype(jnp.float32))
        terms = [states[b] * scale for b in range(seqs)]
        done = [[] for _ in range(seqs)]
        for _ in range(chunk // ROWS):
            parts = [[] for _ in range(seqs)]
            for _ in range(ROWS):
                for b in range(seqs):
                    parts[b].append(fold(terms[b]))
                    terms[b] = terms[b] * keep
            for b in range(seqs):
                done[b].append(merge_rows(parts[b]))
        for b in range(seqs):
            mixed = jnp.concatenate(done[b], axis=0) + fresh_ref[b, pl.ds(first, chunk), :]
            if len(out_ref.shape) == 4:
                own = out_ref.shape[2]
                spot = pl.ds(pl.multiple_of(lax.rem(first, own), chunk), chunk)
                out_ref[lax.div(first, own), b, spot, :] = mixed.astype(jnp.bfloat16)
            else:
                out_ref[b, pl.ds(first, chunk), :] = mixed.astype(jnp.bfloat16)
        return 0

    lax.fori_loop(0, span // chunk, step, 0)


def body(history, lengths, token_ids, embed, residue, decay, skip):
    devices = lax.axis_size("ctx")
    me = lax.axis_index("ctx")
    seqs, tile, width = history.shape
    modes = decay.shape[0]
    gen = token_ids.shape[1]
    total_len = float(tile * devices)
    team = devices // 2
    chips = team // 2
    block = width // team
    lanes = lanes_of(block)
    pieces = block // lanes
    span = gen // 2
    own = gen // devices
    half = me // team
    mine = lax.rem(me, 2) * chips + lax.rem(me, team) // 2
    where = jnp.stack([me, half, mine]).astype(jnp.int32)
    f32 = jnp.float32

    swapped = lax.ppermute(history, "ctx", [(j, j ^ 1) for j in range(devices)])

    rows = embed.shape[0]
    halves = [[h * team + p for p in range(team)] for h in range(2)]
    opposite = [(j, (j + team) % devices) for j in range(devices)]
    columns = embed.reshape(rows, 2, chips, block).transpose(2, 1, 0, 3).reshape(team, rows, block)
    table = lax.all_to_all(columns, "ctx", 0, 0, tiled=True, axis_index_groups=halves)
    table = table.reshape(team * rows, block)
    table_far = lax.ppermute(table, "ctx", opposite)

    part = lambda g, at, ln: (0, 0, lax.rem(at[0], 2) * chips + g)
    partial = pl.pallas_call(
        lambda *refs: history_kernel(total_len, *refs),
        grid_spec=pltpu.PrefetchScalarGridSpec(
            num_scalar_prefetch=2,
            grid=(chips,),
            in_specs=[
                pl.BlockSpec((seqs, tile, block), part),
                pl.BlockSpec((seqs, tile, block), part),
                pl.BlockSpec((modes, block), lambda g, at, ln: part(g, at, ln)[1:]),
            ],
            out_specs=pl.BlockSpec((1, seqs, modes, block), lambda g, at, ln: (g, 0, 0, 0)),
            scratch_shapes=[pltpu.VMEM((2, seqs, tile, block), f32)],
        ),
        out_shape=jax.ShapeDtypeStruct((chips, seqs, modes, block), f32),
        cost_estimate=pl.CostEstimate(
            flops=4 * seqs * tile * modes * block * chips, bytes_accessed=3 * 2**20, transcendentals=0
        ),
        compiler_params=pltpu.CompilerParams(vmem_limit_bytes=16 * 2**20),
        name="history_states",
    )(where, lengths, history, swapped, decay)
    sides = [[h * team + 2 * q + c for q in range(chips)] for h in range(2) for c in range(2)]
    gathered = lax.all_to_all(partial, "ctx", 0, 0, tiled=True, axis_index_groups=sides)
    near = jnp.sum(gathered, axis=0)
    far = lax.ppermute(near, "ctx", opposite)

    strip = lambda g, at: (0, at[2] * pieces + g)
    fresh = pl.pallas_call(
        lambda *refs: fresh_kernel(total_len, *refs),
        grid_spec=pltpu.PrefetchScalarGridSpec(
            num_scalar_prefetch=1,
            grid=(pieces,),
            in_specs=[
                pl.BlockSpec((seqs, gen), lambda g, at: (0, 0)),
                pl.BlockSpec((team * rows, lanes), lambda g, at: (0, g)),
                pl.BlockSpec((team * rows, lanes), lambda g, at: (0, g)),
                pl.BlockSpec((modes, lanes), strip),
                pl.BlockSpec((modes, lanes), strip),
                pl.BlockSpec((1, lanes), strip),
            ],
            out_specs=pl.BlockSpec((seqs, span, lanes), lambda g, at: (0, 0, g)),
            scratch_shapes=[pltpu.VMEM((seqs, gen, lanes), f32)],
        ),
        out_shape=jax.ShapeDtypeStruct((seqs, span, block), f32),
        cost_estimate=pl.CostEstimate(
            flops=6 * seqs * span * modes * block, bytes_accessed=2**21, transcendentals=0
        ),
        compiler_params=pltpu.CompilerParams(vmem_limit_bytes=16 * 2**20),
        name="fresh_scan",
    )(where, token_ids, table, table_far, decay, residue, skip.reshape(1, width))

    direct = own % (2 * ROWS) == 0
    state = pl.BlockSpec((seqs, modes, lanes), lambda g, at: (0, 0, g))
    if direct:
        out_shape = (team, seqs, own, block)
        out_spec = pl.BlockSpec((team, seqs, own, lanes), lambda g, at: (0, 0, 0, g))
    else:
        out_shape = (seqs, span, block)
        out_spec = pl.BlockSpec((seqs, span, lanes), lambda g, at: (0, 0, g))
    mixed = pl.pallas_call(
        lambda *refs: mix_kernel(total_len, *refs),
        grid_spec=pltpu.PrefetchScalarGridSpec(
            num_scalar_prefetch=1,
            grid=(pieces,),
            in_specs=[
                state,
                state,
                pl.BlockSpec((seqs, span, lanes), lambda g, at: (0, 0, g)),
                pl.BlockSpec((modes, lanes), strip),
                pl.BlockSpec((modes, lanes), strip),
            ],
            out_specs=out_spec,
        ),
        out_shape=jax.ShapeDtypeStruct(out_shape, jnp.bfloat16),
        cost_estimate=pl.CostEstimate(
            flops=3 * seqs * span * modes * block, bytes_accessed=2**21, transcendentals=0
        ),
        compiler_params=pltpu.CompilerParams(vmem_limit_bytes=16 * 2**20),
        name="mix_states",
    )(where, near, far, fresh, decay, residue)
    if not direct:
        mixed = mixed.reshape(seqs, team, own, block).transpose(1, 0, 2, 3)
    result = lax.all_to_all(mixed, "ctx", 0, 0, tiled=True, axis_index_groups=halves)
    result = result.reshape(chips, 2, seqs, own, block).transpose(2, 3, 1, 0, 4)
    return result.reshape(seqs, own, width)


def solution(mesh):
    placed = (P("group", "ctx", None), P("group"), P("group", None), P("ctx", None), P(), P(), P())
    return jax.shard_map(
        body, mesh=mesh, in_specs=placed, out_specs=P("group", "ctx", None), check_vma=False
    )
```

```python
import jax
import jax.numpy as jnp
from jax import lax
from jax.experimental import pallas as pl
from jax.experimental.pallas import tpu as pltpu
from jax.sharding import PartitionSpec as P

ROWS = 8
CHUNK = 16
VMEM = 16 * 2**20
f32 = jnp.float32


def lanes_of(block):
    return 256 if block % 256 == 0 else block


def lost(rate):
    series = jnp.ones_like(rate)
    for k in range(12, 1, -1):
        series = 1.0 - rate * series * (1.0 / k)
    return jnp.where(rate < 0.5, rate * series, 1.0 - jnp.exp(-rate))


def merge_rows(parts):
    row = lax.broadcasted_iota(jnp.int32, parts[0].shape, 0)
    low = row < 4
    level = [
        jnp.where(low, parts[i], parts[i + 4]) + pltpu.roll(jnp.where(low, parts[i + 4], parts[i]), 4, 0)
        for i in range(4)
    ]
    for gap in (2, 1):
        first = (row & gap) == 0
        level = [
            jnp.where(first, level[i], level[i + gap])
            + jnp.where(first, pltpu.roll(level[i], 8 - gap, 0), pltpu.roll(level[i + gap], gap, 0))
            for i in range(gap)
        ]
    return level[0]


def fold(x):
    total = x[:ROWS]
    for start in range(ROWS, x.shape[0], ROWS):
        total = total + x[start : start + ROWS]
    return total


def spread_kernel(total_len, me_ref, embed_ref, decay_ref, residue_ref, skip_ref, columns_ref, coef_ref, gain_ref):
    count, _, block = columns_ref.shape
    team = count // 2
    for p in range(team):
        piece = embed_ref[:, p * block : (p + 1) * block]
        columns_ref[p] = piece
        columns_ref[team + p] = piece
    rate = decay_ref[...] / total_len
    keep = jnp.exp(-rate)
    square = keep * keep
    fourth = square * square
    power = fourth * fourth * fourth * square * keep
    coef_ref[0] = rate
    coef_ref[1] = keep
    coef_ref[2] = -float(CHUNK) * ((keep - 1.0) + lost(rate)) * power
    coef_ref[3] = residue_ref[...]
    gain_ref[...] = skip_ref[...]


def history_kernel(total_len, me_ref, lengths_ref, own_ref, other_ref, decay_ref, out_ref, wide):
    seqs, tile, block = own_ref.shape
    me = me_ref[0]
    partner = me + 1 - 2 * lax.rem(me, 2)
    row = lax.broadcasted_iota(jnp.int32, (tile, block), 0)
    for side, (ref, owner) in enumerate(((own_ref, me), (other_ref, partner))):
        for b in range(seqs):
            left = lengths_ref[b] - owner * tile
            wide[side, b] = jnp.where(row < left, ref[b].astype(f32), 0.0)
    lanes = lanes_of(block)
    for start in range(0, block, lanes):
        at = slice(start, start + lanes)
        rate = decay_ref[:, at] / total_len
        keep = jnp.exp(-rate)
        chains = [(side, b) for side in range(2) for b in range(seqs)]

        def step(s, sums):
            return tuple(
                keep * total + wide[side, b, pl.ds(s, 1), at] for (side, b), total in zip(chains, sums)
            )

        zero = jnp.zeros(rate.shape, f32)
        sums = lax.fori_loop(0, tile, step, (zero,) * len(chains), unroll=8)
        for b in range(seqs):
            total = zero
            for side, owner in enumerate((me, partner)):
                after = jnp.maximum(lengths_ref[b] - (owner + 1) * tile, -tile) + 1
                total = total + sums[side * seqs + b] * jnp.exp(-rate * after.astype(f32))
            out_ref[0, b, :, at] = total


def fresh_kernel(team, me_ref, tokens_ref, table_ref, coef_ref, skip_ref, out_ref, fresh):
    seqs, gen = tokens_ref.shape
    span = out_ref.shape[1]
    entry = lax.broadcasted_iota(jnp.int32, (table_ref.shape[0], gen), 0)
    for b in range(seqs):
        chosen = jnp.where(entry == tokens_ref[b : b + 1, :], 1.0, 0.0).astype(jnp.bfloat16)
        fresh[b] = lax.dot_general(
            chosen, table_ref[...], (((0,), (0,)), ((), ())), preferred_element_type=f32
        )
    keep, missed, residue = coef_ref[1], coef_ref[2], coef_ref[3]
    skip = skip_ref[...]
    skipped = lax.div(me_ref[0], team) * span

    def before(index, sums):
        ends = []
        for b, begun in enumerate(sums):
            total = begun
            for j in range(CHUNK):
                total = keep * total + fresh[b, pl.ds(index * CHUNK + j, 1), :]
            ends.append(total + missed * begun)
        return tuple(ends)

    def after(index, sums):
        first = pl.multiple_of(skipped + index * CHUNK, CHUNK)
        local = pl.multiple_of(index * CHUNK, CHUNK)
        ends = []
        for b, begun in enumerate(sums):
            total = begun
            for start in range(0, CHUNK, ROWS):
                parts = []
                for j in range(start, start + ROWS):
                    total = keep * total + fresh[b, pl.ds(first + j, 1), :]
                    parts.append(fold(residue * total))
                direct = skip * fresh[b, pl.ds(first + start, ROWS), :]
                out_ref[b, pl.ds(local + start, ROWS), :] = merge_rows(parts) + direct
            ends.append(total + missed * begun)
        return tuple(ends)

    zero = jnp.zeros(keep.shape, f32)
    sums = lax.fori_loop(0, lax.div(skipped, CHUNK), before, (zero,) * seqs)
    lax.fori_loop(0, span // CHUNK, after, sums)


def mix_kernel(team, me_ref, near_ref, far_ref, fresh_ref, coef_ref, out_ref):
    seqs, span, _ = fresh_ref.shape
    rate, keep, residue = coef_ref[0], coef_ref[1], coef_ref[3]
    states = [residue * (near_ref[b] + far_ref[b]) for b in range(seqs)]
    skipped = lax.div(me_ref[0], team) * span

    def step(index, _):
        first = pl.multiple_of(index * CHUNK, CHUNK)
        scale = jnp.exp(-rate * (skipped + first).astype(f32))
        for b in range(seqs):
            terms = states[b] * scale
            done = []
            for start in range(0, CHUNK, ROWS):
                parts = []
                for j in range(start, start + ROWS):
                    parts.append(fold(terms))
                    if j < CHUNK - 1:
                        terms = terms * keep
                done.append(merge_rows(parts))
            mixed = (jnp.concatenate(done, axis=0) + fresh_ref[b, pl.ds(first, CHUNK), :]).astype(jnp.bfloat16)
            if len(out_ref.shape) == 4:
                own = out_ref.shape[2]
                spot = pl.ds(pl.multiple_of(lax.rem(first, own), CHUNK), CHUNK)
                out_ref[lax.div(first, own), b, spot, :] = mixed
            else:
                out_ref[b, pl.ds(first, CHUNK), :] = mixed
        return 0

    lax.fori_loop(0, span // CHUNK, step, 0)


def join_kernel(mixed_ref, out_ref):
    count, seqs, _, block = mixed_ref.shape
    for p in range(count):
        for b in range(seqs):
            out_ref[b, :, p * block : (p + 1) * block] = mixed_ref[p, b]


def call(kernel, grid, scalars, in_specs, out_specs, out_shape, flops, moved, scratch=()):
    return pl.pallas_call(
        kernel,
        grid_spec=pltpu.PrefetchScalarGridSpec(
            num_scalar_prefetch=scalars,
            grid=grid,
            in_specs=in_specs,
            out_specs=out_specs,
            scratch_shapes=scratch,
        ),
        out_shape=out_shape,
        cost_estimate=pl.CostEstimate(flops=flops, bytes_accessed=moved, transcendentals=0),
        compiler_params=pltpu.CompilerParams(vmem_limit_bytes=VMEM),
    )


def reverse_bits(value, bits):
    result = 0
    for k in range(bits):
        result = result + lax.rem(lax.div(value, 2**k), 2) * 2 ** (bits - 1 - k)
    return result


def body(history, lengths, token_ids, embed, residue, decay, skip):
    devices = lax.axis_size("ctx")
    me = lax.axis_index("ctx")
    seqs, tile, width = history.shape
    modes = decay.shape[0]
    rows = embed.shape[0]
    gen = token_ids.shape[1]
    total_len = float(tile * devices)
    team = devices // 2
    chips = team // 2
    bits = chips.bit_length() - 1
    assert devices == 4 * 2**bits
    block = width // team
    lanes = lanes_of(block)
    pieces = block // lanes
    span = gen // 2
    own = gen // devices
    place = me.astype(jnp.int32).reshape(1)
    chip = lax.rem(me, team) // 2
    opposite = [(j, (j + team) % devices) for j in range(devices)]
    shape = jax.ShapeDtypeStruct

    def paired(x, distance):
        return lax.ppermute(x, "ctx", [(j, j ^ distance) for j in range(devices)])

    swapped = paired(history, 1)

    strip = lambda g, at: (0, lax.rem(at[0], team))
    columns, coef, gain = call(
        lambda *refs: spread_kernel(total_len, *refs),
        (1,),
        1,
        [
            pl.BlockSpec((rows, width), lambda g, at: (0, 0)),
            pl.BlockSpec((modes, block), strip),
            pl.BlockSpec((modes, block), strip),
            pl.BlockSpec((1, block), strip),
        ],
        [
            pl.BlockSpec((devices, rows, block), lambda g, at: (0, 0, 0)),
            pl.BlockSpec((4, modes, block), lambda g, at: (0, 0, 0)),
            pl.BlockSpec((1, block), lambda g, at: (0, 0)),
        ],
        [
            shape((devices, rows, block), jnp.bfloat16),
            shape((4, modes, block), f32),
            shape((1, block), f32),
        ],
        10**5,
        2**20,
    )(place, embed, decay, residue, skip.reshape(1, width))
    table = lax.all_to_all(columns, "ctx", 0, 0, tiled=True)
    table = table.reshape(devices * rows, block)

    def states_for(flip):
        def part(g, at, ln):
            low = lax.rem(at[0], 4)
            if flip:
                low = lax.rem(low + 2, 4)
            return 0, 0, 4 * g + low

        return call(
            lambda *refs: history_kernel(total_len, *refs),
            (chips // 2,),
            2,
            [
                pl.BlockSpec((seqs, tile, block), part),
                pl.BlockSpec((seqs, tile, block), part),
                pl.BlockSpec((modes, block), lambda g, at, ln: part(g, at, ln)[1:]),
            ],
            pl.BlockSpec((1, seqs, modes, block), lambda g, at, ln: (reverse_bits(g, bits - 1), 0, 0, 0)),
            shape((chips // 2, seqs, modes, block), f32),
            2 * seqs * tile * modes * block * chips,
            2**20,
            [pltpu.VMEM((2, seqs, tile, block), f32)],
        )(place, lengths, history, swapped, decay)

    sent = states_for(True)
    came = paired(sent, 2)
    states = states_for(False) + came
    for k in range(1, bits):
        bit = lax.rem(lax.div(chip, 2**k), 2)
        size = states.shape[0] // 2
        sent = lax.dynamic_slice_in_dim(states, (1 - bit) * size, size, 0)
        came = paired(sent, 2 << k)
        states = lax.dynamic_slice_in_dim(states, bit * size, size, 0) + came
    near = states[0]
    far = lax.ppermute(near, "ctx", opposite)

    piece2 = lambda g, at: (0, g)
    piece3 = lambda g, at: (0, 0, g)
    fresh = call(
        lambda *refs: fresh_kernel(team, *refs),
        (pieces,),
        1,
        [
            pl.BlockSpec((seqs, gen), lambda g, at: (0, 0)),
            pl.BlockSpec((devices * rows, lanes), piece2),
            pl.BlockSpec((4, modes, lanes), piece3),
            pl.BlockSpec((1, lanes), piece2),
        ],
        pl.BlockSpec((seqs, span, lanes), piece3),
        shape((seqs, span, block), f32),
        6 * seqs * span * modes * block,
        2**21,
        [pltpu.VMEM((seqs, gen, lanes), f32)],
    )(place, token_ids, table, coef, gain)

    direct = own % CHUNK == 0
    if direct:
        mixed_shape = (team, seqs, own, block)
        mixed_spec = pl.BlockSpec((team, seqs, own, lanes), lambda g, at: (0, 0, 0, g))
    else:
        mixed_shape = (seqs, span, block)
        mixed_spec = pl.BlockSpec((seqs, span, lanes), piece3)
    mixed = call(
        lambda *refs: mix_kernel(team, *refs),
        (pieces,),
        1,
        [
            pl.BlockSpec((seqs, modes, lanes), piece3),
            pl.BlockSpec((seqs, modes, lanes), piece3),
            pl.BlockSpec((seqs, span, lanes), piece3),
            pl.BlockSpec((4, modes, lanes), piece3),
        ],
        mixed_spec,
        shape(mixed_shape, jnp.bfloat16),
        3 * seqs * span * modes * block,
        2**21,
    )(place, near, far, fresh, coef)
    if not direct:
        mixed = mixed.reshape(seqs, team, own, block).transpose(1, 0, 2, 3)
    halves = [[h * team + p for p in range(team)] for h in range(2)]
    result = lax.all_to_all(mixed, "ctx", 0, 0, tiled=True, axis_index_groups=halves)
    parts = 4
    return call(
        join_kernel,
        (parts,),
        0,
        [pl.BlockSpec((team // parts, seqs, own, block), lambda g: (g, 0, 0, 0))],
        pl.BlockSpec((seqs, own, width // parts), lambda g: (0, 0, g)),
        shape((seqs, own, width), jnp.bfloat16),
        10**5,
        2**20,
    )(result)


def solution(mesh):
    placed = (P("group", "ctx", None), P("group"), P("group", None), P("ctx", None), P(), P(), P())
    return jax.shard_map(
        body, mesh=mesh, in_specs=placed, out_specs=P("group", "ctx", None), check_vma=False
    )
```

```python
import jax
import jax.numpy as jnp
from jax import lax
from jax.experimental import pallas as pl
from jax.experimental.pallas import tpu as pltpu
from jax.sharding import PartitionSpec as P

ROWS = 8
CHUNK = 16
VMEM = 16 * 2**20
f32 = jnp.float32


def lanes_of(block):
    return 256 if block % 256 == 0 else block


def lost(rate):
    series = jnp.ones_like(rate)
    for k in range(12, 1, -1):
        series = 1.0 - rate * series * (1.0 / k)
    return jnp.where(rate < 0.5, rate * series, 1.0 - jnp.exp(-rate))


def merge_rows(parts):
    row = lax.broadcasted_iota(jnp.int32, parts[0].shape, 0)
    low = row < 4
    level = [
        jnp.where(low, parts[i], parts[i + 4]) + pltpu.roll(jnp.where(low, parts[i + 4], parts[i]), 4, 0)
        for i in range(4)
    ]
    for gap in (2, 1):
        first = (row & gap) == 0
        level = [
            jnp.where(first, level[i], level[i + gap])
            + jnp.where(first, pltpu.roll(level[i], 8 - gap, 0), pltpu.roll(level[i + gap], gap, 0))
            for i in range(gap)
        ]
    return level[0]


def fold(x):
    total = x[:ROWS]
    for start in range(ROWS, x.shape[0], ROWS):
        total = total + x[start : start + ROWS]
    return total


def spread_kernel(total_len, me_ref, embed_ref, decay_ref, residue_ref, skip_ref, columns_ref, coef_ref, gain_ref):
    count, _, block = columns_ref.shape
    team = count // 2
    for p in range(team):
        piece = embed_ref[:, p * block : (p + 1) * block]
        columns_ref[p] = piece
        columns_ref[team + p] = piece
    rate = decay_ref[...] / total_len
    keep = jnp.exp(-rate)
    square = keep * keep
    fourth = square * square
    power = fourth * fourth * fourth * square * keep
    coef_ref[0] = rate
    coef_ref[1] = keep
    coef_ref[2] = -float(CHUNK) * ((keep - 1.0) + lost(rate)) * power
    coef_ref[3] = residue_ref[...]
    gain_ref[...] = skip_ref[...]


def history_kernel(total_len, me_ref, lengths_ref, own_ref, other_ref, decay_ref, out_ref, wide):
    seqs, tile, block = own_ref.shape
    me = me_ref[0]
    partner = me + 1 - 2 * lax.rem(me, 2)
    row = lax.broadcasted_iota(jnp.int32, (tile, block), 0)
    for side, (ref, owner) in enumerate(((own_ref, me), (other_ref, partner))):
        for b in range(seqs):
            left = lengths_ref[b] - owner * tile
            wide[side, b] = jnp.where(row < left, ref[b].astype(f32), 0.0)
    lanes = lanes_of(block)
    for start in range(0, block, lanes):
        at = slice(start, start + lanes)
        rate = decay_ref[:, at] / total_len
        keep = jnp.exp(-rate)
        chains = [(side, b) for side in range(2) for b in range(seqs)]

        def step(s, sums):
            return tuple(
                keep * total + wide[side, b, pl.ds(s, 1), at] for (side, b), total in zip(chains, sums)
            )

        zero = jnp.zeros(rate.shape, f32)
        sums = lax.fori_loop(0, tile, step, (zero,) * len(chains), unroll=8)
        for b in range(seqs):
            total = zero
            for side, owner in enumerate((me, partner)):
                after = jnp.maximum(lengths_ref[b] - (owner + 1) * tile, -tile) + 1
                total = total + sums[side * seqs + b] * jnp.exp(-rate * after.astype(f32))
            out_ref[0, b, :, at] = total


def fresh_kernel(team, me_ref, tokens_ref, table_ref, coef_ref, skip_ref, out_ref, fresh):
    seqs, gen = tokens_ref.shape
    span = out_ref.shape[1]
    entry = lax.broadcasted_iota(jnp.int32, (table_ref.shape[0], gen), 0)
    for b in range(seqs):
        chosen = jnp.where(entry == tokens_ref[b : b + 1, :], 1.0, 0.0).astype(jnp.bfloat16)
        fresh[b] = lax.dot_general(
            chosen, table_ref[...], (((0,), (0,)), ((), ())), preferred_element_type=f32
        )
    keep, missed, residue = coef_ref[1], coef_ref[2], coef_ref[3]
    skip = skip_ref[...]
    skipped = lax.div(me_ref[0], team) * span

    def before(index, sums):
        ends = []
        for b, begun in enumerate(sums):
            total = begun
            for j in range(CHUNK):
                total = keep * total + fresh[b, pl.ds(index * CHUNK + j, 1), :]
            ends.append(total + missed * begun)
        return tuple(ends)

    def after(index, sums):
        first = pl.multiple_of(skipped + index * CHUNK, CHUNK)
        local = pl.multiple_of(index * CHUNK, CHUNK)
        ends = []
        for b, begun in enumerate(sums):
            total = begun
            for start in range(0, CHUNK, ROWS):
                parts = []
                for j in range(start, start + ROWS):
                    total = keep * total + fresh[b, pl.ds(first + j, 1), :]
                    parts.append(fold(residue * total))
                direct = skip * fresh[b, pl.ds(first + start, ROWS), :]
                out_ref[b, pl.ds(local + start, ROWS), :] = merge_rows(parts) + direct
            ends.append(total + missed * begun)
        return tuple(ends)

    zero = jnp.zeros(keep.shape, f32)
    sums = lax.fori_loop(0, lax.div(skipped, CHUNK), before, (zero,) * seqs)
    lax.fori_loop(0, span // CHUNK, after, sums)


def mix_kernel(team, me_ref, near_ref, far_ref, fresh_ref, coef_ref, out_ref):
    seqs, span, _ = fresh_ref.shape
    rate, keep, residue = coef_ref[0], coef_ref[1], coef_ref[3]
    states = [residue * (near_ref[b] + far_ref[b]) for b in range(seqs)]
    skipped = lax.div(me_ref[0], team) * span

    def step(index, _):
        first = pl.multiple_of(index * CHUNK, CHUNK)
        scale = jnp.exp(-rate * (skipped + first).astype(f32))
        for b in range(seqs):
            terms = states[b] * scale
            done = []
            for start in range(0, CHUNK, ROWS):
                parts = []
                for j in range(start, start + ROWS):
                    parts.append(fold(terms))
                    if j < CHUNK - 1:
                        terms = terms * keep
                done.append(merge_rows(parts))
            mixed = (jnp.concatenate(done, axis=0) + fresh_ref[b, pl.ds(first, CHUNK), :]).astype(jnp.bfloat16)
            if len(out_ref.shape) == 4:
                own = out_ref.shape[2]
                spot = pl.ds(pl.multiple_of(lax.rem(first, own), CHUNK), CHUNK)
                out_ref[lax.div(first, own), b, spot, :] = mixed
            else:
                out_ref[b, pl.ds(first, CHUNK), :] = mixed
        return 0

    lax.fori_loop(0, span // CHUNK, step, 0)


def join_kernel(mixed_ref, out_ref):
    count, seqs, _, block = mixed_ref.shape
    for p in range(count):
        for b in range(seqs):
            out_ref[b, :, p * block : (p + 1) * block] = mixed_ref[p, b]


def call(kernel, grid, scalars, in_specs, out_specs, out_shape, flops, moved, scratch=()):
    return pl.pallas_call(
        kernel,
        grid_spec=pltpu.PrefetchScalarGridSpec(
            num_scalar_prefetch=scalars,
            grid=grid,
            in_specs=in_specs,
            out_specs=out_specs,
            scratch_shapes=scratch,
        ),
        out_shape=out_shape,
        cost_estimate=pl.CostEstimate(flops=flops, bytes_accessed=moved, transcendentals=0),
        compiler_params=pltpu.CompilerParams(vmem_limit_bytes=VMEM),
    )


def reverse_bits(value, bits):
    result = 0
    for k in range(bits):
        result = result + lax.rem(lax.div(value, 2**k), 2) * 2 ** (bits - 1 - k)
    return result


def body(history, lengths, token_ids, embed, residue, decay, skip):
    devices = lax.axis_size("ctx")
    me = lax.axis_index("ctx")
    seqs, tile, width = history.shape
    modes = decay.shape[0]
    rows = embed.shape[0]
    gen = token_ids.shape[1]
    total_len = float(tile * devices)
    team = devices // 2
    chips = team // 2
    bits = chips.bit_length() - 1
    assert devices == 4 * 2**bits
    block = width // team
    lanes = lanes_of(block)
    pieces = block // lanes
    span = gen // 2
    own = gen // devices
    place = me.astype(jnp.int32).reshape(1)
    history, embed, residue, decay, skip = (
        pltpu.with_memory_space_constraint(x, pltpu.HBM)
        for x in (history, embed, residue, decay, skip.reshape(1, width))
    )
    chip = lax.rem(me, team) // 2
    opposite = [(j, (j + team) % devices) for j in range(devices)]
    shape = jax.ShapeDtypeStruct

    def paired(x, distance):
        return lax.ppermute(x, "ctx", [(j, j ^ distance) for j in range(devices)])

    swapped = pltpu.with_memory_space_constraint(paired(history, 1), pltpu.VMEM)

    strip = lambda g, at: (0, lax.rem(at[0], team))
    columns, coef, gain = call(
        lambda *refs: spread_kernel(total_len, *refs),
        (1,),
        1,
        [
            pl.BlockSpec((rows, width), lambda g, at: (0, 0)),
            pl.BlockSpec((modes, block), strip),
            pl.BlockSpec((modes, block), strip),
            pl.BlockSpec((1, block), strip),
        ],
        [
            pl.BlockSpec((devices, rows, block), lambda g, at: (0, 0, 0)),
            pl.BlockSpec((4, modes, block), lambda g, at: (0, 0, 0)),
            pl.BlockSpec((1, block), lambda g, at: (0, 0)),
        ],
        [
            shape((devices, rows, block), jnp.bfloat16),
            shape((4, modes, block), f32),
            shape((1, block), f32),
        ],
        10**5,
        2**20,
    )(place, embed, decay, residue, skip)
    table = lax.all_to_all(columns, "ctx", 0, 0, tiled=True)
    table = table.reshape(devices * rows, block)

    def states_for(flip):
        def part(g, at, ln):
            low = lax.rem(at[0], 4)
            if flip:
                low = lax.rem(low + 2, 4)
            return 0, 0, 4 * g + low

        return call(
            lambda *refs: history_kernel(total_len, *refs),
            (chips // 2,),
            2,
            [
                pl.BlockSpec((seqs, tile, block), part),
                pl.BlockSpec((seqs, tile, block), part),
                pl.BlockSpec((modes, block), lambda g, at, ln: part(g, at, ln)[1:]),
            ],
            pl.BlockSpec((1, seqs, modes, block), lambda g, at, ln: (reverse_bits(g, bits - 1), 0, 0, 0)),
            shape((chips // 2, seqs, modes, block), f32),
            2 * seqs * tile * modes * block * chips,
            2**20,
            [pltpu.VMEM((2, seqs, tile, block), f32)],
        )(place, lengths, history, swapped, decay)

    sent = states_for(True)
    came = paired(sent, 2)
    states = states_for(False) + came
    for k in range(1, bits):
        bit = lax.rem(lax.div(chip, 2**k), 2)
        size = states.shape[0] // 2
        sent = lax.dynamic_slice_in_dim(states, (1 - bit) * size, size, 0)
        came = paired(sent, 2 << k)
        states = lax.dynamic_slice_in_dim(states, bit * size, size, 0) + came
    near = states[0]
    far = lax.ppermute(near, "ctx", opposite)

    piece2 = lambda g, at: (0, g)
    piece3 = lambda g, at: (0, 0, g)
    fresh = call(
        lambda *refs: fresh_kernel(team, *refs),
        (pieces,),
        1,
        [
            pl.BlockSpec((seqs, gen), lambda g, at: (0, 0)),
            pl.BlockSpec((devices * rows, lanes), piece2),
            pl.BlockSpec((4, modes, lanes), piece3),
            pl.BlockSpec((1, lanes), piece2),
        ],
        pl.BlockSpec((seqs, span, lanes), piece3),
        shape((seqs, span, block), f32),
        6 * seqs * span * modes * block,
        2**21,
        [pltpu.VMEM((seqs, gen, lanes), f32)],
    )(place, token_ids, table, coef, gain)

    direct = own % CHUNK == 0
    if direct:
        mixed_shape = (team, seqs, own, block)
        mixed_spec = pl.BlockSpec((team, seqs, own, lanes), lambda g, at: (0, 0, 0, g))
    else:
        mixed_shape = (seqs, span, block)
        mixed_spec = pl.BlockSpec((seqs, span, lanes), piece3)
    mixed = call(
        lambda *refs: mix_kernel(team, *refs),
        (pieces,),
        1,
        [
            pl.BlockSpec((seqs, modes, lanes), piece3),
            pl.BlockSpec((seqs, modes, lanes), piece3),
            pl.BlockSpec((seqs, span, lanes), piece3),
            pl.BlockSpec((4, modes, lanes), piece3),
        ],
        mixed_spec,
        shape(mixed_shape, jnp.bfloat16),
        3 * seqs * span * modes * block,
        2**21,
    )(place, near, far, fresh, coef)
    if not direct:
        mixed = mixed.reshape(seqs, team, own, block).transpose(1, 0, 2, 3)
    halves = [[h * team + p for p in range(team)] for h in range(2)]
    result = lax.all_to_all(mixed, "ctx", 0, 0, tiled=True, axis_index_groups=halves)
    parts = 4
    return call(
        join_kernel,
        (parts,),
        0,
        [pl.BlockSpec((team // parts, seqs, own, block), lambda g: (g, 0, 0, 0))],
        pl.BlockSpec((seqs, own, width // parts), lambda g: (0, 0, g)),
        shape((seqs, own, width), jnp.bfloat16),
        10**5,
        2**20,
    )(result)


def solution(mesh):
    placed = (P("group", "ctx", None), P("group"), P("group", None), P("ctx", None), P(), P(), P())
    return jax.shard_map(
        body, mesh=mesh, in_specs=placed, out_specs=P("group", "ctx", None), check_vma=False
    )
```

```python
import jax
import jax.numpy as jnp
from jax import lax
from jax.experimental import pallas as pl
from jax.experimental.pallas import tpu as pltpu
from jax.sharding import PartitionSpec as P

ROWS = 8
CHUNK = 16
VMEM = 16 * 2**20
f32 = jnp.float32


def lanes_of(block):
    return 256 if block % 256 == 0 else block


def lost(rate):
    series = jnp.ones_like(rate)
    for k in range(12, 1, -1):
        series = 1.0 - rate * series * (1.0 / k)
    return jnp.where(rate < 0.5, rate * series, 1.0 - jnp.exp(-rate))


def reverse_bits(value, bits):
    result = 0
    for k in range(bits):
        result = result + lax.rem(lax.div(value, 2**k), 2) * 2 ** (bits - 1 - k)
    return result


def merge_rows(parts):
    row = lax.broadcasted_iota(jnp.int32, parts[0].shape, 0)
    low = row < 4
    level = [
        jnp.where(low, parts[i], parts[i + 4]) + pltpu.roll(jnp.where(low, parts[i + 4], parts[i]), 4, 0)
        for i in range(4)
    ]
    for gap in (2, 1):
        first = (row & gap) == 0
        level = [
            jnp.where(first, level[i], level[i + gap])
            + jnp.where(first, pltpu.roll(level[i], 8 - gap, 0), pltpu.roll(level[i + gap], gap, 0))
            for i in range(gap)
        ]
    return level[0]


def fold(x):
    total = x[:ROWS]
    for start in range(ROWS, x.shape[0], ROWS):
        total = total + x[start : start + ROWS]
    return total


def horner(keep, rows_of, count, tile):
    def step(s, sums):
        return tuple(keep * total + rows_of(i, s) for i, total in enumerate(sums))

    return lax.fori_loop(0, tile, step, (jnp.zeros(keep.shape, f32),) * count, unroll=16)


def low_bits(me, flip):
    low = lax.rem(me, 4)
    return lax.rem(low + 2, 4) if flip else low


def masked(value, length, start):
    row = lax.broadcasted_iota(jnp.int32, value.shape, 0)
    return jnp.where(row < length - start, value.astype(f32), 0.0)


def lift(rate, length, end, tile):
    return jnp.exp(-rate * (jnp.maximum(length - end, -tile) + 1).astype(f32))


def prepare_kernel(
    total_len, bits, me_ref, lengths_ref, embed_ref, history_ref, all_decay_ref, decay_ref, residue_ref, skip_ref,
    columns_ref, coef_ref, gain_ref, states_ref, rates_ref,
    entries, pieces, wide, load_sem, piece_sem, rate_sem, store_sem,
):
    count, _, block = columns_ref.shape
    team = count // 2
    chips = team // 2
    seqs, tile, _ = history_ref.shape
    me = me_ref[0]

    def origin(spot):
        low = lax.rem(lax.rem(me, 4) + lax.select(spot < chips // 2, 2, 0), 4)
        return 4 * reverse_bits(lax.rem(spot, chips // 2), bits - 1) + low

    def piece_copies(spot):
        at = pl.ds(pl.multiple_of(origin(spot) * block, block), block)
        return (
            pltpu.make_async_copy(history_ref.at[:, :, at], pieces.at[spot], piece_sem.at[spot]),
            pltpu.make_async_copy(all_decay_ref.at[:, at], rates_ref.at[spot], rate_sem.at[spot]),
        )

    load = pltpu.make_async_copy(embed_ref, entries, load_sem)
    load.start()

    @pl.loop(0, chips)
    def _(spot):
        for copy in piece_copies(spot):
            copy.start()

    rate = decay_ref[...] / total_len
    keep = jnp.exp(-rate)
    square = keep * keep
    fourth = square * square
    power = fourth * fourth * fourth * square * keep
    coef_ref[0] = rate
    coef_ref[1] = keep
    coef_ref[2] = -float(CHUNK) * ((keep - 1.0) + lost(rate)) * power
    coef_ref[3] = residue_ref[...]
    gain_ref[...] = skip_ref[...]

    def store(p):
        at = pl.ds(pl.multiple_of(lax.rem(p, team) * block, block), block)
        return pltpu.make_async_copy(entries.at[:, at], columns_ref.at[p], store_sem.at[p])

    load.wait()

    @pl.loop(0, count)
    def _(p):
        store(p).start()

    @pl.loop(0, chips)
    def _(spot):
        for copy in piece_copies(spot):
            copy.wait()
        rate = rates_ref[spot] / total_len
        rates_ref[spot] = rate
        keep = jnp.exp(-rate)
        for b in range(seqs):
            wide[b] = masked(pieces[spot, b], lengths_ref[b], me * tile)
        sums = horner(keep, lambda b, s: wide[b, pl.ds(s, 1), :], seqs, tile)
        for b in range(seqs):
            states_ref[spot, b] = sums[b] * lift(rate, lengths_ref[b], (me + 1) * tile, tile)

    @pl.loop(0, count)
    def _(p):
        store(p).wait()


def partner_kernel(flip, bits, me_ref, lengths_ref, other_ref, states_ref, rates_ref, out_ref, wide):
    seqs, tile, _ = other_ref.shape
    half, _, _, block = out_ref.shape
    me = me_ref[0]
    partner = me + 1 - 2 * lax.rem(me, 2)
    base = 0 if flip else half

    @pl.loop(0, half)
    def _(spot):
        start = (4 * reverse_bits(spot, bits - 1) + low_bits(me, flip)) * block
        at = pl.ds(pl.multiple_of(start, block), block)
        rate = rates_ref[base + spot]
        keep = jnp.exp(-rate)
        for b in range(seqs):
            wide[b] = masked(other_ref[b, :, at], lengths_ref[b], partner * tile)
        sums = horner(keep, lambda b, s: wide[b, pl.ds(s, 1), :], seqs, tile)
        for b in range(seqs):
            out_ref[spot, b] = states_ref[base + spot, b] + sums[b] * lift(
                rate, lengths_ref[b], (partner + 1) * tile, tile
            )


def fresh_kernel(team, me_ref, chosen_ref, table_ref, coef_ref, skip_ref, out_ref, fresh):
    seqs = chosen_ref.shape[0]
    span = out_ref.shape[1]
    for b in range(seqs):
        fresh[b] = jnp.dot(chosen_ref[b], table_ref[...], preferred_element_type=f32)
    keep, missed, residue = coef_ref[1], coef_ref[2], coef_ref[3]
    skip = skip_ref[...]
    skipped = lax.div(me_ref[0], team) * span

    def before(index, sums):
        ends = []
        for b, begun in enumerate(sums):
            total = begun
            for j in range(CHUNK):
                total = keep * total + fresh[b, pl.ds(index * CHUNK + j, 1), :]
            ends.append(total + missed * begun)
        return tuple(ends)

    def after(index, sums):
        first = pl.multiple_of(skipped + index * CHUNK, CHUNK)
        local = pl.multiple_of(index * CHUNK, CHUNK)
        ends = []
        for b, begun in enumerate(sums):
            total = begun
            for start in range(0, CHUNK, ROWS):
                parts = []
                for j in range(start, start + ROWS):
                    total = keep * total + fresh[b, pl.ds(first + j, 1), :]
                    parts.append(fold(residue * total))
                direct = skip * fresh[b, pl.ds(first + start, ROWS), :]
                out_ref[b, pl.ds(local + start, ROWS), :] = merge_rows(parts) + direct
            ends.append(total + missed * begun)
        return tuple(ends)

    zero = jnp.zeros(keep.shape, f32)
    sums = lax.fori_loop(0, lax.div(skipped, CHUNK), before, (zero,) * seqs)
    lax.fori_loop(0, span // CHUNK, after, sums)


def mix_kernel(team, me_ref, near_ref, far_ref, fresh_ref, coef_ref, out_ref):
    seqs, span, _ = fresh_ref.shape
    rate, keep, residue = coef_ref[0], coef_ref[1], coef_ref[3]
    states = [residue * (near_ref[b] + far_ref[b]) for b in range(seqs)]
    skipped = lax.div(me_ref[0], team) * span

    def step(index, _):
        first = pl.multiple_of(index * CHUNK, CHUNK)
        scale = jnp.exp(-rate * (skipped + first).astype(f32))
        for b in range(seqs):
            terms = states[b] * scale
            done = []
            for start in range(0, CHUNK, ROWS):
                parts = []
                for j in range(start, start + ROWS):
                    parts.append(fold(terms))
                    if j < CHUNK - 1:
                        terms = terms * keep
                done.append(merge_rows(parts))
            mixed = (jnp.concatenate(done, axis=0) + fresh_ref[b, pl.ds(first, CHUNK), :]).astype(jnp.bfloat16)
            if len(out_ref.shape) == 4:
                own = out_ref.shape[2]
                spot = pl.ds(pl.multiple_of(lax.rem(first, own), CHUNK), CHUNK)
                out_ref[lax.div(first, own), b, spot, :] = mixed
            else:
                out_ref[b, pl.ds(first, CHUNK), :] = mixed
        return 0

    lax.fori_loop(0, span // CHUNK, step, 0)


def join_kernel(mixed_ref, out_ref):
    count, seqs, _, block = mixed_ref.shape
    for p in range(count):
        for b in range(seqs):
            out_ref[b, :, p * block : (p + 1) * block] = mixed_ref[p, b]


def call(kernel, grid, scalars, in_specs, out_specs, out_shape, flops, moved, scratch=()):
    return pl.pallas_call(
        kernel,
        grid_spec=pltpu.PrefetchScalarGridSpec(
            num_scalar_prefetch=scalars,
            grid=grid,
            in_specs=in_specs,
            out_specs=out_specs,
            scratch_shapes=scratch,
        ),
        out_shape=out_shape,
        cost_estimate=pl.CostEstimate(flops=flops, bytes_accessed=moved, transcendentals=0),
        compiler_params=pltpu.CompilerParams(vmem_limit_bytes=VMEM),
    )


def body(history, lengths, token_ids, embed, residue, decay, skip):
    devices = lax.axis_size("ctx")
    me = lax.axis_index("ctx")
    seqs, tile, width = history.shape
    modes = decay.shape[0]
    rows = embed.shape[0]
    gen = token_ids.shape[1]
    total_len = float(tile * devices)
    team = devices // 2
    chips = team // 2
    bits = chips.bit_length() - 1
    assert devices == 4 * 2**bits
    block = width // team
    lanes = lanes_of(block)
    pieces = block // lanes
    span = gen // 2
    own = gen // devices
    place = me.astype(jnp.int32).reshape(1)
    history, embed, residue, decay, skip, lengths = (
        pltpu.with_memory_space_constraint(x, pltpu.HBM)
        for x in (history, embed, residue, decay, skip.reshape(1, width), lengths)
    )
    chip = lax.rem(me, team) // 2
    opposite = [(j, (j + team) % devices) for j in range(devices)]
    shape = jax.ShapeDtypeStruct

    def paired(x, distance):
        return lax.ppermute(x, "ctx", [(j, j ^ distance) for j in range(devices)])

    swapped = pltpu.with_memory_space_constraint(paired(history, 1), pltpu.VMEM)

    strip = lambda g, at, ln: (0, lax.rem(at[0], team))
    hbm = pl.BlockSpec(memory_space=pltpu.HBM)
    vmem = pl.BlockSpec(memory_space=pltpu.VMEM)
    columns, coef, gain, states, rates = call(
        lambda *refs: prepare_kernel(total_len, bits, *refs),
        (1,),
        2,
        [
            hbm,
            hbm,
            hbm,
            pl.BlockSpec((modes, block), strip),
            pl.BlockSpec((modes, block), strip),
            pl.BlockSpec((1, block), strip),
        ],
        [hbm, vmem, vmem, vmem, vmem],
        [
            shape((devices, rows, block), jnp.bfloat16),
            shape((4, modes, block), f32),
            shape((1, block), f32),
            shape((chips, seqs, modes, block), f32),
            shape((chips, modes, block), f32),
        ],
        2 * seqs * tile * modes * block * chips,
        2**20,
        [
            pltpu.VMEM((rows, width), jnp.bfloat16),
            pltpu.VMEM((chips, seqs, tile, block), jnp.bfloat16),
            pltpu.VMEM((seqs, tile, block), f32),
            pltpu.SemaphoreType.DMA(()),
            pltpu.SemaphoreType.DMA((chips,)),
            pltpu.SemaphoreType.DMA((chips,)),
            pltpu.SemaphoreType.DMA((devices,)),
        ],
    )(place, lengths, embed, history, decay, decay, residue, skip)
    table = lax.all_to_all(columns, "ctx", 0, 0, tiled=True)
    table = table.reshape(devices * rows, block)

    def finish(flip):
        return call(
            lambda *refs: partner_kernel(flip, bits, *refs),
            (1,),
            2,
            [vmem] * 3,
            vmem,
            shape((chips // 2, seqs, modes, block), f32),
            seqs * tile * modes * block * chips,
            2**20,
            [pltpu.VMEM((seqs, tile, block), f32)],
        )(place, lengths, swapped, states, rates)

    sent = finish(True)
    came = paired(sent, 2)
    mine = finish(False) + came
    done = 1
    while done < bits:
        now = min(2, bits - done)
        ways, size = 2**now, mine.shape[0] // 2**now
        digit = lax.rem(lax.div(chip, 2**done), ways)
        take = lambda x, d: lax.dynamic_slice_in_dim(x, reverse_bits(d, now) * size, size, 0)
        total = take(mine, digit)
        for d in range(1, ways):
            flipped = digit ^ d
            total = total + paired(take(mine, flipped), d << (done + 1))
        mine = total
        done += now
    near = mine[0]
    far = lax.ppermute(near, "ctx", opposite)

    entry = lax.broadcasted_iota(jnp.int32, (seqs, gen, devices * rows), 2)
    chosen = (token_ids[:, :, None] == entry).astype(jnp.bfloat16)
    piece2 = lambda g, at: (0, g)
    piece3 = lambda g, at: (0, 0, g)
    fresh = call(
        lambda *refs: fresh_kernel(team, *refs),
        (pieces,),
        1,
        [
            pl.BlockSpec((seqs, gen, devices * rows), lambda g, at: (0, 0, 0)),
            pl.BlockSpec((devices * rows, lanes), piece2),
            pl.BlockSpec((4, modes, lanes), piece3),
            pl.BlockSpec((1, lanes), piece2),
        ],
        pl.BlockSpec((seqs, span, lanes), piece3),
        shape((seqs, span, block), f32),
        6 * seqs * span * modes * block,
        2**21,
        [pltpu.VMEM((seqs, gen, lanes), f32)],
    )(place, chosen, table, coef, gain)

    direct = own % CHUNK == 0
    if direct:
        mixed_shape = (team, seqs, own, block)
        mixed_spec = pl.BlockSpec((team, seqs, own, lanes), lambda g, at: (0, 0, 0, g))
    else:
        mixed_shape = (seqs, span, block)
        mixed_spec = pl.BlockSpec((seqs, span, lanes), piece3)
    mixed = call(
        lambda *refs: mix_kernel(team, *refs),
        (pieces,),
        1,
        [
            pl.BlockSpec((seqs, modes, lanes), piece3),
            pl.BlockSpec((seqs, modes, lanes), piece3),
            pl.BlockSpec((seqs, span, lanes), piece3),
            pl.BlockSpec((4, modes, lanes), piece3),
        ],
        mixed_spec,
        shape(mixed_shape, jnp.bfloat16),
        3 * seqs * span * modes * block,
        2**21,
    )(place, near, far, fresh, coef)
    if not direct:
        mixed = mixed.reshape(seqs, team, own, block).transpose(1, 0, 2, 3)
    halves = [[h * team + p for p in range(team)] for h in range(2)]
    result = lax.all_to_all(mixed, "ctx", 0, 0, tiled=True, axis_index_groups=halves)
    parts = 4
    return call(
        join_kernel,
        (parts,),
        0,
        [pl.BlockSpec((team // parts, seqs, own, block), lambda g: (g, 0, 0, 0))],
        pl.BlockSpec((seqs, own, width // parts), lambda g: (0, 0, g)),
        shape((seqs, own, width), jnp.bfloat16),
        10**5,
        2**20,
    )(result)


def solution(mesh):
    placed = (P("group", "ctx", None), P("group"), P("group", None), P("ctx", None), P(), P(), P())
    return jax.shard_map(
        body, mesh=mesh, in_specs=placed, out_specs=P("group", "ctx", None), check_vma=False
    )
```

```python
import jax
import jax.numpy as jnp
from jax import lax
from jax.experimental import pallas as pl
from jax.experimental.pallas import tpu as pltpu
from jax.sharding import PartitionSpec as P

ROWS = 8
CHUNK = 16
LANES = 128
VMEM = 16 * 2**20
f32 = jnp.float32


def reverse_bits(value, bits):
    result = 0
    for k in range(bits):
        result = result + lax.rem(lax.div(value, 2**k), 2) * 2 ** (bits - 1 - k)
    return result


def reversed_int(value, bits):
    return sum((value >> k & 1) << (bits - 1 - k) for k in range(bits))


def merge_rows(parts):
    row = lax.broadcasted_iota(jnp.int32, parts[0].shape, 0)
    low = row < 4
    level = [
        jnp.where(low, parts[i], parts[i + 4]) + pltpu.roll(jnp.where(low, parts[i + 4], parts[i]), 4, 0)
        for i in range(4)
    ]
    for gap in (2, 1):
        first = (row & gap) == 0
        level = [
            jnp.where(first, level[i], level[i + gap])
            + jnp.where(first, pltpu.roll(level[i], 8 - gap, 0), pltpu.roll(level[i + gap], gap, 0))
            for i in range(gap)
        ]
    return level[0]


def fold(x):
    total = x[:ROWS]
    for start in range(ROWS, x.shape[0], ROWS):
        total = total + x[start : start + ROWS]
    return total


def horner(keep, rows_of, count, tile):
    def step(s, sums):
        return tuple(keep * total + rows_of(i, s) for i, total in enumerate(sums))

    return lax.fori_loop(0, tile, step, (jnp.zeros(keep.shape, f32),) * count, unroll=16)


def low_bits(me, flip):
    low = lax.rem(me, 4)
    return lax.rem(low + 2, 4) if flip else low


def masked(value, length, start):
    row = lax.broadcasted_iota(jnp.int32, value.shape, 0)
    return jnp.where(row < length - start, value.astype(f32), 0.0)


def lift(rate, length, end, tile):
    return jnp.exp(-rate * (jnp.maximum(length - end, -tile) + 1).astype(f32))


def prepare_kernel(
    total_len, bits, me_ref, lengths_ref, embed_ref, history_ref, decay_ref,
    columns_ref, states_ref, rates_ref,
    entries, pieces, wide, load_sem, piece_sem, rate_sem, store_sem,
):
    count, _, block = columns_ref.shape
    team = count // 2
    chips = team // 2
    seqs, tile, _ = history_ref.shape
    me = me_ref[0]

    def piece_copies(spot):
        low = low_bits(me, spot < chips // 2)
        start = (4 * reversed_int(spot % (chips // 2), bits - 1) + low) * block
        at = pl.ds(pl.multiple_of(start, block), block)
        return (
            pltpu.make_async_copy(history_ref.at[:, :, at], pieces.at[spot], piece_sem.at[spot]),
            pltpu.make_async_copy(decay_ref.at[:, at], rates_ref.at[spot], rate_sem.at[spot]),
        )

    load = pltpu.make_async_copy(embed_ref, entries, load_sem)
    load.start()
    for spot in range(chips):
        for copy in piece_copies(spot):
            copy.start()
    stores = [
        pltpu.make_async_copy(entries.at[:, pl.ds(p % team * block, block)], columns_ref.at[p], store_sem.at[p])
        for p in range(count)
    ]
    load.wait()
    for copy in stores:
        copy.start()

    @pl.loop(0, chips)
    def _(spot):
        for source, target, sem in ((history_ref, pieces, piece_sem), (decay_ref, rates_ref, rate_sem)):
            origin = source.at[:, :, pl.ds(0, block)] if len(source.shape) == 3 else source.at[:, pl.ds(0, block)]
            pltpu.make_async_copy(origin, target.at[spot], sem.at[spot]).wait()
        rate = rates_ref[spot] / total_len
        rates_ref[spot] = rate
        keep = jnp.exp(-rate)
        for b in range(seqs):
            wide[b] = masked(pieces[spot, b], lengths_ref[b], me * tile)
        sums = horner(keep, lambda b, s: wide[b, pl.ds(s, 1), :], seqs, tile)
        for b in range(seqs):
            states_ref[spot, b] = sums[b] * lift(rate, lengths_ref[b], (me + 1) * tile, tile)

    for copy in stores:
        copy.wait()


def partner_kernel(flip, bits, me_ref, lengths_ref, other_ref, states_ref, rates_ref, out_ref, wide):
    seqs, tile, _ = other_ref.shape
    half, _, _, block = out_ref.shape
    me = me_ref[0]
    partner = me + 1 - 2 * lax.rem(me, 2)
    base = 0 if flip else half

    @pl.loop(0, half)
    def _(spot):
        start = (4 * reverse_bits(spot, bits - 1) + low_bits(me, flip)) * block
        at = pl.ds(pl.multiple_of(start, block), block)
        rate = rates_ref[base + spot]
        keep = jnp.exp(-rate)
        for b in range(seqs):
            wide[b] = masked(other_ref[b, :, at], lengths_ref[b], partner * tile)
        sums = horner(keep, lambda b, s: wide[b, pl.ds(s, 1), :], seqs, tile)
        for b in range(seqs):
            out_ref[spot, b] = states_ref[base + spot, b] + sums[b] * lift(
                rate, lengths_ref[b], (partner + 1) * tile, tile
            )


def tables_kernel(total_len, team, span, me_ref, decay_ref, residue_ref, skip_ref, weights_ref, taps_ref, keeps_ref, ages_ref):
    modes, block = decay_ref.shape
    rate = decay_ref[...] / total_len
    residue = residue_ref[...]
    taps = []
    for i in range(CHUNK):
        weight = residue * jnp.exp(-rate * float(i))
        weights_ref[i] = weight
        taps.append(fold(weight))
    for start in range(0, CHUNK, ROWS):
        taps_ref[start : start + ROWS] = merge_rows(taps[start : start + ROWS])
    taps_ref[0:1] = taps_ref[0:1] + skip_ref[...]
    keeps_ref[0] = jnp.exp(-rate)
    keeps_ref[1] = jnp.exp(-rate * float(CHUNK))
    keeps_ref[2] = rate
    chunks = span // CHUNK
    begin = (lax.div(me_ref[0], team) * span).astype(f32)
    times = begin + float(CHUNK) * lax.broadcasted_iota(jnp.int32, (chunks, block), 0).astype(f32)

    @pl.loop(0, modes)
    def _(k):
        ages_ref[k] = jnp.exp(-keeps_ref[2, pl.ds(k, 1), :] * times)


def chunk_rows(group, offset):
    return pl.ds(group * ROWS * CHUNK + offset, ROWS, stride=CHUNK)


def fresh_kernel(team, me_ref, chosen_ref, table_ref, taps_ref, keeps_ref, conv_ref, carry_ref, fresh, ends):
    seqs, _, _ = chosen_ref.shape
    tiles, span = conv_ref.shape[1:3]
    modes = keeps_ref.shape[1]
    chunks = span // CHUNK
    late = lax.div(me_ref[0], team)
    strips = [(b, t) for t in range(tiles) for b in range(seqs)]

    def look_up(begin):
        for b in range(seqs):
            rows = chosen_ref[b, pl.ds(pl.multiple_of(begin, span), span), :]
            found = jnp.dot(rows, table_ref[...], preferred_element_type=f32)
            for t in range(tiles):
                fresh[b, t] = found[:, t * LANES : (t + 1) * LANES]

    def lanes(t):
        return slice(t * LANES, (t + 1) * LANES)

    def finish_chunks(values, b, t, group):
        for k in range(modes):
            keep = jnp.broadcast_to(keeps_ref[0, k : k + 1, lanes(t)], (ROWS, LANES))
            total = keep * values[0]
            for value in values[1:]:
                total = keep * (total + value)
            ends[b, t, chunk_rows(group, k), :] = total

    def values_of(b, t, group):
        return [fresh[b, t, chunk_rows(group, i), :] for i in range(CHUNK)]

    def rows_of(chunk):
        return pl.ds(pl.multiple_of(chunk * modes, modes), modes)

    for b, t in strips:
        carry_ref[b, t, 0:modes, :] = jnp.zeros((modes, LANES), f32)

    @pl.when(late == 1)
    def _():
        look_up(0)

        @pl.loop(0, chunks // ROWS)
        def _(group):
            for b, t in strips:
                finish_chunks(values_of(b, t, group), b, t, group)

        def advance(chunk, carries):
            return tuple(
                keeps_ref[1, :, lanes(t)] * carry + ends[b, t, rows_of(chunk), :] for (b, t), carry in zip(strips, carries)
            )

        carries = lax.fori_loop(0, chunks, advance, (jnp.zeros((modes, LANES), f32),) * len(strips))
        for (b, t), carry in zip(strips, carries):
            carry_ref[b, t, 0:modes, :] = carry

    look_up(late * span)

    @pl.loop(0, chunks // ROWS)
    def _(group):
        for b, t in strips:
            values = values_of(b, t, group)
            taps = [jnp.broadcast_to(taps_ref[d : d + 1, lanes(t)], (ROWS, LANES)) for d in range(CHUNK)]
            for i in range(CHUNK):
                total = taps[0] * values[i]
                for d in range(1, i + 1):
                    total = total + taps[d] * values[i - d]
                conv_ref[b, t, chunk_rows(group, i), :] = total
            finish_chunks(values, b, t, group)

    @pl.loop(1, chunks)
    def _(chunk):
        for b, t in strips:
            old, new = rows_of(chunk - 1), rows_of(chunk)
            carry_ref[b, t, new, :] = keeps_ref[1, :, lanes(t)] * carry_ref[b, t, old, :] + ends[b, t, old, :]


def mix_kernel(near_ref, far_ref, conv_ref, carry_ref, weights_ref, ages_ref, out_ref, state, total_ref):
    seqs, tiles, span, _ = conv_ref.shape
    modes = near_ref.shape[1]
    chunks = span // CHUNK
    for b in range(seqs):
        state[b] = near_ref[b] + far_ref[b]

    @pl.loop(0, chunks // ROWS)
    def _(group):
        old = pl.ds(pl.multiple_of(group * ROWS, ROWS), ROWS)
        for t in range(tiles):
            at = slice(t * LANES, (t + 1) * LANES)
            begun = [
                [
                    carry_ref[b, t, chunk_rows(group, k), :] + ages_ref[k, old, at] * state[b, k : k + 1, at]
                    for k in range(modes)
                ]
                for b in range(seqs)
            ]
            for i in range(CHUNK):
                weights = [weights_ref[i, k : k + 1, at] for k in range(modes)]
                for b in range(seqs):
                    total = conv_ref[b, t, chunk_rows(group, i), :]
                    other = weights[0] * begun[b][0]
                    for k in range(1, modes):
                        if k % 2:
                            total = total + weights[k] * begun[b][k]
                        else:
                            other = other + weights[k] * begun[b][k]
                    total_ref[b, t, chunk_rows(0, i), :] = total + other
        for chunk in range(ROWS):
            first = pl.multiple_of((group * ROWS + chunk) * CHUNK, CHUNK)
            for b, t in ((b, t) for b in range(seqs) for t in range(tiles)):
                at = slice(t * LANES, (t + 1) * LANES)
                mixed = total_ref[b, t, chunk * CHUNK : (chunk + 1) * CHUNK, :].astype(jnp.bfloat16)
                if len(out_ref.shape) == 4:
                    own = out_ref.shape[2]
                    spot = pl.ds(pl.multiple_of(lax.rem(first, own), CHUNK), CHUNK)
                    out_ref[lax.div(first, own), b, spot, at] = mixed
                else:
                    out_ref[b, pl.ds(first, CHUNK), at] = mixed


def join_kernel(mixed_ref, out_ref):
    count, seqs, _, block = mixed_ref.shape
    for p in range(count):
        for b in range(seqs):
            out_ref[b, :, p * block : (p + 1) * block] = mixed_ref[p, b]


def call(kernel, grid, scalars, in_specs, out_specs, out_shape, flops, moved, scratch=()):
    return pl.pallas_call(
        kernel,
        grid_spec=pltpu.PrefetchScalarGridSpec(
            num_scalar_prefetch=scalars,
            grid=grid,
            in_specs=in_specs,
            out_specs=out_specs,
            scratch_shapes=scratch,
        ),
        out_shape=out_shape,
        cost_estimate=pl.CostEstimate(flops=flops, bytes_accessed=moved, transcendentals=0),
        compiler_params=pltpu.CompilerParams(vmem_limit_bytes=VMEM),
    )


def body(history, lengths, token_ids, embed, residue, decay, skip):
    devices = lax.axis_size("ctx")
    me = lax.axis_index("ctx")
    seqs, tile, width = history.shape
    modes = decay.shape[0]
    rows = embed.shape[0]
    gen = token_ids.shape[1]
    total_len = float(tile * devices)
    team = devices // 2
    chips = team // 2
    bits = chips.bit_length() - 1
    assert devices == 4 * 2**bits
    block = width // team
    span = gen // 2
    chunks = span // CHUNK
    tiles = block // LANES
    assert block % LANES == 0 and span % (ROWS * CHUNK) == 0
    own = gen // devices
    place = me.astype(jnp.int32).reshape(1)
    history, embed, residue, decay, skip, lengths = (
        pltpu.with_memory_space_constraint(x, pltpu.HBM)
        for x in (history, embed, residue, decay, skip.reshape(1, width), lengths)
    )
    chip = lax.rem(me, team) // 2
    opposite = [(j, (j + team) % devices) for j in range(devices)]
    shape = jax.ShapeDtypeStruct

    def paired(x, distance):
        return lax.ppermute(x, "ctx", [(j, j ^ distance) for j in range(devices)])

    swapped = pltpu.with_memory_space_constraint(paired(history, 1), pltpu.VMEM)

    hbm = pl.BlockSpec(memory_space=pltpu.HBM)
    vmem = pl.BlockSpec(memory_space=pltpu.VMEM)
    columns, states, rates = call(
        lambda *refs: prepare_kernel(total_len, bits, *refs),
        (1,),
        2,
        [hbm] * 3,
        [hbm, vmem, vmem],
        [
            shape((devices, rows, block), jnp.bfloat16),
            shape((chips, seqs, modes, block), f32),
            shape((chips, modes, block), f32),
        ],
        2 * seqs * tile * modes * block * chips,
        2**20,
        [
            pltpu.VMEM((rows, width), jnp.bfloat16),
            pltpu.VMEM((chips, seqs, tile, block), jnp.bfloat16),
            pltpu.VMEM((seqs, tile, block), f32),
            pltpu.SemaphoreType.DMA(()),
            pltpu.SemaphoreType.DMA((chips,)),
            pltpu.SemaphoreType.DMA((chips,)),
            pltpu.SemaphoreType.DMA((devices,)),
        ],
    )(place, lengths, embed, history, decay)
    table = lax.all_to_all(columns, "ctx", 0, 0, tiled=True)
    table = table.reshape(devices * rows, block)

    def finish(flip):
        return call(
            lambda *refs: partner_kernel(flip, bits, *refs),
            (1,),
            2,
            [vmem] * 3,
            vmem,
            shape((chips // 2, seqs, modes, block), f32),
            seqs * tile * modes * block * chips,
            2**20,
            [pltpu.VMEM((seqs, tile, block), f32)],
        )(place, lengths, swapped, states, rates)

    sent = finish(True)
    came = paired(sent, 2)
    mine = finish(False) + came
    done = 1
    while done < bits:
        now = min(2, bits - done)
        ways, size = 2**now, mine.shape[0] // 2**now
        digit = lax.rem(lax.div(chip, 2**done), ways)
        take = lambda x, d: lax.dynamic_slice_in_dim(x, reverse_bits(d, now) * size, size, 0)
        total = take(mine, digit)
        for d in range(1, ways):
            flipped = digit ^ d
            total = total + paired(take(mine, flipped), d << (done + 1))
        mine = total
        done += now
    near = mine[0]
    far = lax.ppermute(near, "ctx", opposite)

    entry = lax.broadcasted_iota(jnp.int32, (seqs, gen, devices * rows), 2)
    chosen = (token_ids[:, :, None] == entry).astype(jnp.bfloat16)
    strip = lambda g, at: (0, lax.rem(at[0], team))
    weights, taps, keeps, ages = call(
        lambda *refs: tables_kernel(total_len, team, span, *refs),
        (1,),
        1,
        [pl.BlockSpec((modes, block), strip)] * 2 + [pl.BlockSpec((1, block), strip)],
        [vmem] * 4,
        [
            shape((CHUNK, modes, block), f32),
            shape((CHUNK, block), f32),
            shape((3, modes, block), f32),
            shape((modes, chunks, block), f32),
        ],
        10**6,
        2**20,
    )(place, decay, residue, skip)
    conv, carry = call(
        lambda *refs: fresh_kernel(team, *refs),
        (1,),
        1,
        [vmem] * 4,
        [vmem] * 2,
        [shape((seqs, tiles, span, LANES), f32), shape((seqs, tiles, chunks * modes, LANES), f32)],
        6 * seqs * span * modes * block,
        2**21,
        [pltpu.VMEM((seqs, tiles, span, LANES), f32), pltpu.VMEM((seqs, tiles, chunks * modes, LANES), f32)],
    )(place, chosen, table, taps, keeps)

    direct = own % CHUNK == 0
    mixed = call(
        mix_kernel,
        (1,),
        0,
        [vmem] * 6,
        vmem,
        shape((team, seqs, own, block) if direct else (seqs, span, block), jnp.bfloat16),
        3 * seqs * span * modes * block,
        2**21,
        [pltpu.VMEM((seqs, modes, block), f32), pltpu.VMEM((seqs, tiles, ROWS * CHUNK, LANES), f32)],
    )(near, far, conv, carry, weights, ages)
    if not direct:
        mixed = mixed.reshape(seqs, team, own, block).transpose(1, 0, 2, 3)
    halves = [[h * team + p for p in range(team)] for h in range(2)]
    result = lax.all_to_all(mixed, "ctx", 0, 0, tiled=True, axis_index_groups=halves)
    parts = 4
    return call(
        join_kernel,
        (parts,),
        0,
        [pl.BlockSpec((team // parts, seqs, own, block), lambda g: (g, 0, 0, 0))],
        pl.BlockSpec((seqs, own, width // parts), lambda g: (0, 0, g)),
        shape((seqs, own, width), jnp.bfloat16),
        10**5,
        2**20,
    )(result)


def solution(mesh):
    placed = (P("group", "ctx", None), P("group"), P("group", None), P("ctx", None), P(), P(), P())
    return jax.shard_map(body, mesh=mesh, in_specs=placed, out_specs=P("group", "ctx", None), check_vma=False)
```

```python
import jax
import jax.numpy as jnp
from jax import lax
from jax.experimental import pallas as pl
from jax.experimental.pallas import tpu as pltpu
from jax.sharding import PartitionSpec as P

ROWS = 8
CHUNK = 16
LANES = 128
VMEM = 16 * 2**20
f32 = jnp.float32


def reverse_bits(value, bits):
    result = 0
    for k in range(bits):
        result = result + lax.rem(lax.div(value, 2**k), 2) * 2 ** (bits - 1 - k)
    return result


def merge_rows(parts):
    row = lax.broadcasted_iota(jnp.int32, parts[0].shape, 0)
    low = row < 4
    level = [
        jnp.where(low, parts[i], parts[i + 4]) + pltpu.roll(jnp.where(low, parts[i + 4], parts[i]), 4, 0)
        for i in range(4)
    ]
    for gap in (2, 1):
        first = (row & gap) == 0
        level = [
            jnp.where(first, level[i], level[i + gap])
            + jnp.where(first, pltpu.roll(level[i], 8 - gap, 0), pltpu.roll(level[i + gap], gap, 0))
            for i in range(gap)
        ]
    return level[0]


def fold(x):
    total = x[:ROWS]
    for start in range(ROWS, x.shape[0], ROWS):
        total = total + x[start : start + ROWS]
    return total


def horner(keep, rows_of, count, tile):
    def step(s, sums):
        return tuple(keep * total + rows_of(i, s) for i, total in enumerate(sums))

    return lax.fori_loop(0, tile, step, (jnp.zeros(keep.shape, f32),) * count, unroll=16)


def block_of(me, spot, give, bits):
    core = lax.rem(me, 2)
    top = lax.rem(lax.div(me, 2**bits), 2)
    if give:
        top = 1 - top
    return 2 * (top * 2 ** (bits - 1) + reverse_bits(spot, bits - 1)) + core


def masked(value, length, start):
    row = lax.broadcasted_iota(jnp.int32, value.shape, 0)
    return jnp.where(row < length - start, value.astype(f32), 0.0)


def lift(rate, length, end, tile):
    return jnp.exp(-rate * (jnp.maximum(length - end, -tile) + 1).astype(f32))


def prepare_kernel(
    total_len, bits, me_ref, lengths_ref, embed_ref, history_ref, decay_ref,
    columns_ref, states_ref, decays_ref, held_ref,
    entries, pieces, wide, load_sem, piece_sem, rate_sem, store_sem,
):
    count, _, block = columns_ref.shape
    half, seqs, tile, _ = pieces.shape
    team = count // 2
    me = me_ref[0]

    def fetch(spot, give):
        start = pl.multiple_of(block_of(me, spot, give, bits) * block, block)
        target, index = (pieces, spot) if give else (held_ref, spot + half)
        return (
            pltpu.make_async_copy(decay_ref.at[:, pl.ds(start, block)], decays_ref.at[index], rate_sem.at[index]),
            pltpu.make_async_copy(history_ref.at[:, :, pl.ds(start, block)], target.at[spot], piece_sem.at[index]),
        )

    copies = [copy for give in (True, False) for spot in range(half) for copy in fetch(spot, give)]
    load = pltpu.make_async_copy(embed_ref, entries, load_sem)
    for copy in copies[: 2 * half]:
        copy.start()
    load.start()
    for copy in copies[2 * half :]:
        copy.start()
    stores = [
        pltpu.make_async_copy(entries.at[:, pl.ds(p % team * block, block)], columns_ref.at[p], store_sem.at[p])
        for p in range(count)
    ]
    load.wait()
    for copy in stores:
        copy.start()
    for copy in copies[: 2 * half]:
        copy.wait()

    @pl.loop(0, half)
    def _(spot):
        rate = decays_ref[spot] / total_len
        sums = partial_states(rate, lambda b: pieces[spot, b], wide, lengths_ref, me * tile)
        for b in range(seqs):
            states_ref[spot, b] = sums[b]

    for copy in copies[2 * half :] + stores:
        copy.wait()


def partial_states(rate, tile_of, wide, lengths_ref, start):
    seqs, tile, _ = wide.shape
    keep = jnp.exp(-rate)
    for b in range(seqs):
        wide[b] = masked(tile_of(b), lengths_ref[b], start)
    sums = horner(keep, lambda b, s: wide[b, pl.ds(s, 1), :], seqs, tile)
    return [sums[b] * lift(rate, lengths_ref[b], start + tile, tile) for b in range(seqs)]


def give_kernel(total_len, bits, me_ref, lengths_ref, other_ref, states_ref, decays_ref, out_ref, wide):
    seqs, tile, block = wide.shape
    me = me_ref[0]
    partner = me + 1 - 2 * lax.rem(me, 2)

    @pl.loop(0, out_ref.shape[0])
    def _(spot):
        at = pl.ds(pl.multiple_of(block_of(me, spot, True, bits) * block, block), block)
        rate = decays_ref[spot] / total_len
        sums = partial_states(rate, lambda b: other_ref[b, :, at], wide, lengths_ref, partner * tile)
        for b in range(seqs):
            out_ref[spot, b] = states_ref[spot, b] + sums[b]


def keep_kernel(total_len, bits, me_ref, lengths_ref, other_ref, held_ref, decays_ref, out_ref, wide):
    seqs, tile, block = wide.shape
    half = out_ref.shape[0]
    me = me_ref[0]
    partner = me + 1 - 2 * lax.rem(me, 2)

    @pl.loop(0, half)
    def _(spot):
        at = pl.ds(pl.multiple_of(block_of(me, spot, False, bits) * block, block), block)
        rate = decays_ref[spot + half] / total_len
        own = partial_states(rate, lambda b: held_ref[spot, b], wide, lengths_ref, me * tile)
        sums = partial_states(rate, lambda b: other_ref[b, :, at], wide, lengths_ref, partner * tile)
        for b in range(seqs):
            out_ref[spot, b] = own[b] + sums[b]


def tables_kernel(total_len, team, span, me_ref, decay_ref, residue_ref, skip_ref, weights_ref, taps_ref, keeps_ref, ages_ref):
    modes, block = decay_ref.shape
    rate = decay_ref[...] / total_len
    residue = residue_ref[...]
    taps = []
    for i in range(CHUNK):
        weight = residue * jnp.exp(-rate * float(i))
        weights_ref[i] = weight
        taps.append(fold(weight))
    for start in range(0, CHUNK, ROWS):
        taps_ref[start : start + ROWS] = merge_rows(taps[start : start + ROWS])
    taps_ref[0:1] = taps_ref[0:1] + skip_ref[...]
    keeps_ref[0] = jnp.exp(-rate)
    keeps_ref[1] = jnp.exp(-rate * float(CHUNK))
    keeps_ref[2] = rate
    chunks = span // CHUNK
    begin = (lax.div(me_ref[0], team) * span).astype(f32)
    times = begin + float(CHUNK) * lax.broadcasted_iota(jnp.int32, (chunks, block), 0).astype(f32)

    @pl.loop(0, modes)
    def _(k):
        ages_ref[k] = jnp.exp(-keeps_ref[2, pl.ds(k, 1), :] * times)


def chunk_rows(group, offset):
    return pl.ds(group * ROWS * CHUNK + offset, ROWS, stride=CHUNK)


def fresh_kernel(team, me_ref, chosen_ref, table_ref, taps_ref, keeps_ref, conv_ref, carry_ref, fresh, ends):
    seqs, _, _ = chosen_ref.shape
    tiles, span = conv_ref.shape[1:3]
    modes = keeps_ref.shape[1]
    chunks = span // CHUNK
    late = lax.div(me_ref[0], team)
    strips = [(b, t) for t in range(tiles) for b in range(seqs)]

    def look_up(begin):
        for b in range(seqs):
            rows = chosen_ref[b, pl.ds(pl.multiple_of(begin, span), span), :]
            found = jnp.dot(rows, table_ref[...], preferred_element_type=f32)
            for t in range(tiles):
                fresh[b, t] = found[:, t * LANES : (t + 1) * LANES]

    def lanes(t):
        return slice(t * LANES, (t + 1) * LANES)

    def finish_chunks(values, b, t, group):
        for k in range(modes):
            keep = jnp.broadcast_to(keeps_ref[0, k : k + 1, lanes(t)], (ROWS, LANES))
            total = keep * values[0]
            for value in values[1:]:
                total = keep * (total + value)
            ends[b, t, chunk_rows(group, k), :] = total

    def values_of(b, t, group):
        return [fresh[b, t, chunk_rows(group, i), :] for i in range(CHUNK)]

    def rows_of(chunk):
        return pl.ds(pl.multiple_of(chunk * modes, modes), modes)

    for b, t in strips:
        carry_ref[b, t, 0:modes, :] = jnp.zeros((modes, LANES), f32)

    @pl.when(late == 1)
    def _():
        look_up(0)

        @pl.loop(0, chunks // ROWS)
        def _(group):
            for b, t in strips:
                finish_chunks(values_of(b, t, group), b, t, group)

        def advance(chunk, carries):
            return tuple(
                keeps_ref[1, :, lanes(t)] * carry + ends[b, t, rows_of(chunk), :] for (b, t), carry in zip(strips, carries)
            )

        carries = lax.fori_loop(0, chunks, advance, (jnp.zeros((modes, LANES), f32),) * len(strips))
        for (b, t), carry in zip(strips, carries):
            carry_ref[b, t, 0:modes, :] = carry

    look_up(late * span)

    @pl.loop(0, chunks // ROWS)
    def _(group):
        for b, t in strips:
            values = values_of(b, t, group)
            taps = [jnp.broadcast_to(taps_ref[d : d + 1, lanes(t)], (ROWS, LANES)) for d in range(CHUNK)]
            for i in range(CHUNK):
                total = taps[0] * values[i]
                for d in range(1, i + 1):
                    total = total + taps[d] * values[i - d]
                conv_ref[b, t, chunk_rows(group, i), :] = total
            finish_chunks(values, b, t, group)

    @pl.loop(1, chunks)
    def _(chunk):
        for b, t in strips:
            old, new = rows_of(chunk - 1), rows_of(chunk)
            carry_ref[b, t, new, :] = keeps_ref[1, :, lanes(t)] * carry_ref[b, t, old, :] + ends[b, t, old, :]


def mix_kernel(near_ref, far_ref, conv_ref, carry_ref, weights_ref, ages_ref, out_ref, state, total_ref):
    seqs, tiles, span, _ = conv_ref.shape
    modes = near_ref.shape[1]
    chunks = span // CHUNK
    for b in range(seqs):
        state[b] = near_ref[b] + far_ref[b]

    @pl.loop(0, chunks // ROWS)
    def _(group):
        old = pl.ds(pl.multiple_of(group * ROWS, ROWS), ROWS)
        for t in range(tiles):
            at = slice(t * LANES, (t + 1) * LANES)
            begun = [
                [
                    carry_ref[b, t, chunk_rows(group, k), :] + ages_ref[k, old, at] * state[b, k : k + 1, at]
                    for k in range(modes)
                ]
                for b in range(seqs)
            ]
            for i in range(CHUNK):
                weights = [weights_ref[i, k : k + 1, at] for k in range(modes)]
                for b in range(seqs):
                    total = conv_ref[b, t, chunk_rows(group, i), :]
                    other = weights[0] * begun[b][0]
                    for k in range(1, modes):
                        if k % 2:
                            total = total + weights[k] * begun[b][k]
                        else:
                            other = other + weights[k] * begun[b][k]
                    total_ref[b, t, chunk_rows(0, i), :] = total + other
        for chunk in range(ROWS):
            first = pl.multiple_of((group * ROWS + chunk) * CHUNK, CHUNK)
            for b, t in ((b, t) for b in range(seqs) for t in range(tiles)):
                at = slice(t * LANES, (t + 1) * LANES)
                mixed = total_ref[b, t, chunk * CHUNK : (chunk + 1) * CHUNK, :].astype(jnp.bfloat16)
                if len(out_ref.shape) == 4:
                    own = out_ref.shape[2]
                    spot = pl.ds(pl.multiple_of(lax.rem(first, own), CHUNK), CHUNK)
                    out_ref[lax.div(first, own), b, spot, at] = mixed
                else:
                    out_ref[b, pl.ds(first, CHUNK), at] = mixed


def join_kernel(mixed_ref, out_ref, sem):
    count, seqs, _, block = mixed_ref.shape
    copies = [
        pltpu.make_async_copy(
            mixed_ref.at[p, b], out_ref.at[b, :, pl.ds(p * block, block)], sem.at[p, b]
        )
        for p in range(count)
        for b in range(seqs)
    ]
    for copy in copies:
        copy.start()
    for copy in copies:
        copy.wait()


def call(kernel, grid, scalars, in_specs, out_specs, out_shape, flops, moved, scratch=()):
    return pl.pallas_call(
        kernel,
        grid_spec=pltpu.PrefetchScalarGridSpec(
            num_scalar_prefetch=scalars,
            grid=grid,
            in_specs=in_specs,
            out_specs=out_specs,
            scratch_shapes=scratch,
        ),
        out_shape=out_shape,
        cost_estimate=pl.CostEstimate(flops=flops, bytes_accessed=moved, transcendentals=0),
        compiler_params=pltpu.CompilerParams(vmem_limit_bytes=VMEM),
    )


def body(history, lengths, token_ids, embed, residue, decay, skip):
    devices = lax.axis_size("ctx")
    me = lax.axis_index("ctx")
    seqs, tile, width = history.shape
    modes = decay.shape[0]
    rows = embed.shape[0]
    gen = token_ids.shape[1]
    total_len = float(tile * devices)
    team = devices // 2
    chips = team // 2
    bits = chips.bit_length() - 1
    assert devices == 4 * 2**bits
    block = width // team
    span = gen // 2
    chunks = span // CHUNK
    tiles = block // LANES
    assert block % LANES == 0 and span % (ROWS * CHUNK) == 0
    own = gen // devices
    place = me.astype(jnp.int32).reshape(1)
    history, embed, residue, decay, skip, lengths = (
        pltpu.with_memory_space_constraint(x, pltpu.HBM)
        for x in (history, embed, residue, decay, skip.reshape(1, width), lengths)
    )
    chip = lax.rem(me, team) // 2
    opposite = [(j, (j + team) % devices) for j in range(devices)]
    shape = jax.ShapeDtypeStruct

    def paired(x, distance):
        return lax.ppermute(x, "ctx", [(j, j ^ distance) for j in range(devices)])

    swapped = pltpu.with_memory_space_constraint(paired(history, 1), pltpu.VMEM)

    hbm = pl.BlockSpec(memory_space=pltpu.HBM)
    vmem = pl.BlockSpec(memory_space=pltpu.VMEM)
    half = chips // 2
    columns, states, decays, held = call(
        lambda *refs: prepare_kernel(total_len, bits, *refs),
        (1,),
        2,
        [hbm] * 3,
        [hbm, vmem, vmem, vmem],
        [
            shape((devices, rows, block), jnp.bfloat16),
            shape((half, seqs, modes, block), f32),
            shape((chips, modes, block), f32),
            shape((half, seqs, tile, block), jnp.bfloat16),
        ],
        2 * seqs * tile * modes * block * half,
        2**20,
        [
            pltpu.VMEM((rows, width), jnp.bfloat16),
            pltpu.VMEM((half, seqs, tile, block), jnp.bfloat16),
            pltpu.VMEM((seqs, tile, block), f32),
            pltpu.SemaphoreType.DMA(()),
            pltpu.SemaphoreType.DMA((chips,)),
            pltpu.SemaphoreType.DMA((chips,)),
            pltpu.SemaphoreType.DMA((devices,)),
        ],
    )(place, lengths, embed, history, decay)
    table = lax.all_to_all(columns, "ctx", 0, 0, tiled=True)
    table = table.reshape(devices * rows, block)

    def finish(kernel, operand, flops):
        return call(
            lambda *refs: kernel(total_len, bits, *refs),
            (1,),
            2,
            [vmem] * 3,
            vmem,
            shape((half, seqs, modes, block), f32),
            flops,
            2**20,
            [pltpu.VMEM((seqs, tile, block), f32)],
        )(place, lengths, swapped, operand, decays)

    work = 2 * seqs * tile * modes * block * half
    sent = finish(give_kernel, states, work)
    came = paired(sent, 2**bits)
    mine = finish(keep_kernel, held, 2 * work) + came
    done = 0
    while done < bits - 1:
        now = min(2, bits - 1 - done)
        ways, size = 2**now, mine.shape[0] // 2**now
        digit = lax.rem(lax.div(chip, 2**done), ways)
        take = lambda x, d: lax.dynamic_slice_in_dim(x, reverse_bits(d, now) * size, size, 0)
        total = take(mine, digit)
        for d in range(1, ways):
            flipped = digit ^ d
            total = total + paired(take(mine, flipped), d << (done + 1))
        mine = total
        done += now
    near = mine[0]
    far = lax.ppermute(near, "ctx", opposite)

    entry = lax.broadcasted_iota(jnp.int32, (seqs, gen, devices * rows), 2)
    chosen = (token_ids[:, :, None] == entry).astype(jnp.bfloat16)
    strip = lambda g, at: (0, lax.rem(at[0], team))
    weights, taps, keeps, ages = call(
        lambda *refs: tables_kernel(total_len, team, span, *refs),
        (1,),
        1,
        [pl.BlockSpec((modes, block), strip)] * 2 + [pl.BlockSpec((1, block), strip)],
        [vmem] * 4,
        [
            shape((CHUNK, modes, block), f32),
            shape((CHUNK, block), f32),
            shape((3, modes, block), f32),
            shape((modes, chunks, block), f32),
        ],
        10**6,
        2**20,
    )(place, decay, residue, skip)
    conv, carry = call(
        lambda *refs: fresh_kernel(team, *refs),
        (1,),
        1,
        [vmem] * 4,
        [vmem] * 2,
        [shape((seqs, tiles, span, LANES), f32), shape((seqs, tiles, chunks * modes, LANES), f32)],
        6 * seqs * span * modes * block,
        2**21,
        [pltpu.VMEM((seqs, tiles, span, LANES), f32), pltpu.VMEM((seqs, tiles, chunks * modes, LANES), f32)],
    )(place, chosen, table, taps, keeps)

    direct = own % CHUNK == 0
    mixed = call(
        mix_kernel,
        (1,),
        0,
        [vmem] * 6,
        vmem,
        shape((team, seqs, own, block) if direct else (seqs, span, block), jnp.bfloat16),
        3 * seqs * span * modes * block,
        2**21,
        [pltpu.VMEM((seqs, modes, block), f32), pltpu.VMEM((seqs, tiles, ROWS * CHUNK, LANES), f32)],
    )(near, far, conv, carry, weights, ages)
    if not direct:
        mixed = mixed.reshape(seqs, team, own, block).transpose(1, 0, 2, 3)
    halves = [[h * team + p for p in range(team)] for h in range(2)]
    result = lax.all_to_all(mixed, "ctx", 0, 0, tiled=True, axis_index_groups=halves)
    return call(
        join_kernel,
        (1,),
        0,
        [vmem],
        hbm,
        shape((seqs, own, width), jnp.bfloat16),
        10**5,
        2**20,
        [pltpu.SemaphoreType.DMA((team, seqs))],
    )(result)


def solution(mesh):
    placed = (P("group", "ctx", None), P("group"), P("group", None), P("ctx", None), P(), P(), P())
    return jax.shard_map(body, mesh=mesh, in_specs=placed, out_specs=P("group", "ctx", None), check_vma=False)
```

```python
import jax
import jax.numpy as jnp
from jax import lax
from jax.experimental import pallas as pl
from jax.experimental.pallas import tpu as pltpu
from jax.sharding import PartitionSpec as P

ROWS = 8
CHUNK = 16
LANES = 128
VMEM = 16 * 2**20
f32 = jnp.float32


def reverse_bits(value, bits):
    result = 0
    for k in range(bits):
        result = result + lax.rem(lax.div(value, 2**k), 2) * 2 ** (bits - 1 - k)
    return result


def merge_rows(parts):
    row = lax.broadcasted_iota(jnp.int32, parts[0].shape, 0)
    low = row < 4
    level = [
        jnp.where(low, parts[i], parts[i + 4]) + pltpu.roll(jnp.where(low, parts[i + 4], parts[i]), 4, 0)
        for i in range(4)
    ]
    for gap in (2, 1):
        first = (row & gap) == 0
        level = [
            jnp.where(first, level[i], level[i + gap])
            + jnp.where(first, pltpu.roll(level[i], 8 - gap, 0), pltpu.roll(level[i + gap], gap, 0))
            for i in range(gap)
        ]
    return level[0]


def fold(x):
    total = x[:ROWS]
    for start in range(ROWS, x.shape[0], ROWS):
        total = total + x[start : start + ROWS]
    return total


def horner(keep, rows_of, count, tile):
    def step(s, sums):
        return tuple(keep * total + rows_of(i, s) for i, total in enumerate(sums))

    return lax.fori_loop(0, tile, step, (jnp.zeros(keep.shape, f32),) * count, unroll=16)


def block_of(me, spot, give, bits):
    core = lax.rem(me, 2)
    top = lax.rem(lax.div(me, 2**bits), 2)
    if give:
        top = 1 - top
    return 2 * (top * 2 ** (bits - 1) + reverse_bits(spot, bits - 1)) + core


def masked(value, length, start):
    row = lax.broadcasted_iota(jnp.int32, value.shape, 0)
    return jnp.where(row < length - start, value.astype(f32), 0.0)


def lift(rate, length, end, tile):
    return jnp.exp(-rate * (jnp.maximum(length - end, -tile) + 1).astype(f32))


def prepare_kernel(
    total_len, bits, lengths_ref, embed_ref, history_ref, decay_ref,
    columns_ref, states_ref, decays_ref, held_ref, ends_ref,
    entries, pieces, wide, lengths, length_sem, load_sem, piece_sem, rate_sem, store_sem,
):
    count, _, block = columns_ref.shape
    half, seqs, tile, _ = pieces.shape
    team = count // 2
    me = lax.axis_index("ctx")

    def fetch(spot, give):
        start = pl.multiple_of(block_of(me, spot, give, bits) * block, block)
        target, index = (pieces, spot) if give else (held_ref, spot + half)
        return (
            pltpu.make_async_copy(decay_ref.at[:, pl.ds(start, block)], decays_ref.at[index], rate_sem.at[index]),
            pltpu.make_async_copy(history_ref.at[:, :, pl.ds(start, block)], target.at[spot], piece_sem.at[index]),
        )

    copies = [copy for give in (True, False) for spot in range(half) for copy in fetch(spot, give)]
    loads = [
        pltpu.make_async_copy(embed_ref.at[:, pl.ds(p * block, block)], entries.at[p], load_sem.at[p])
        for p in range(team)
    ]
    stores = [
        pltpu.make_async_copy(entries, columns_ref.at[pl.ds(h * team, team)], store_sem.at[h]) for h in range(2)
    ]
    length_copy = pltpu.make_async_copy(lengths_ref, lengths, length_sem)
    for copy in [length_copy] + loads + copies:
        copy.start()
    for copy in loads:
        copy.wait()
    for copy in stores:
        copy.start()
    length_copy.wait()
    for b in range(seqs):
        ends_ref[b : b + 1, :] = jnp.full((1, block), lengths[b], jnp.int32)
    for copy in copies[: 2 * half]:
        copy.wait()

    @pl.loop(0, half)
    def _(spot):
        rate = decays_ref[spot] / total_len
        sums = partial_states(rate, lambda b: pieces[spot, b], wide, ends_ref, me * tile)
        for b in range(seqs):
            states_ref[spot, b] = sums[b]

    for copy in copies[2 * half :] + stores:
        copy.wait()


def partial_states(rate, tile_of, wide, ends_ref, start):
    seqs, tile, _ = wide.shape
    keep = jnp.exp(-rate)
    for b in range(seqs):
        wide[b] = masked(tile_of(b), ends_ref[b : b + 1, :], start)
    sums = horner(keep, lambda b, s: wide[b, pl.ds(s, 1), :], seqs, tile)
    return [sums[b] * lift(rate, ends_ref[b : b + 1, :], start + tile, tile) for b in range(seqs)]


def give_kernel(total_len, bits, ends_ref, other_ref, states_ref, decays_ref, out_ref, wide):
    seqs, tile, block = wide.shape
    me = lax.axis_index("ctx")
    partner = me + 1 - 2 * lax.rem(me, 2)

    @pl.loop(0, out_ref.shape[0])
    def _(spot):
        at = pl.ds(pl.multiple_of(block_of(me, spot, True, bits) * block, block), block)
        rate = decays_ref[spot] / total_len
        sums = partial_states(rate, lambda b: other_ref[b, :, at], wide, ends_ref, partner * tile)
        for b in range(seqs):
            out_ref[spot, b] = states_ref[spot, b] + sums[b]


def keep_kernel(total_len, bits, ends_ref, other_ref, held_ref, decays_ref, out_ref, wide):
    seqs, tile, block = wide.shape
    half = out_ref.shape[0]
    me = lax.axis_index("ctx")
    partner = me + 1 - 2 * lax.rem(me, 2)

    @pl.loop(0, half)
    def _(spot):
        at = pl.ds(pl.multiple_of(block_of(me, spot, False, bits) * block, block), block)
        rate = decays_ref[spot + half] / total_len
        own = partial_states(rate, lambda b: held_ref[spot, b], wide, ends_ref, me * tile)
        sums = partial_states(rate, lambda b: other_ref[b, :, at], wide, ends_ref, partner * tile)
        for b in range(seqs):
            out_ref[spot, b] = own[b] + sums[b]


def tables_kernel(total_len, team, span, me_ref, decay_ref, residue_ref, skip_ref, weights_ref, taps_ref, keeps_ref, ages_ref):
    modes, block = decay_ref.shape
    rate = decay_ref[...] / total_len
    residue = residue_ref[...]
    taps = []
    for i in range(CHUNK):
        weight = residue * jnp.exp(-rate * float(i))
        weights_ref[i] = weight
        taps.append(fold(weight))
    for start in range(0, CHUNK, ROWS):
        taps_ref[start : start + ROWS] = merge_rows(taps[start : start + ROWS])
    taps_ref[0:1] = taps_ref[0:1] + skip_ref[...]
    keeps_ref[0] = jnp.exp(-rate)
    keeps_ref[1] = jnp.exp(-rate * float(CHUNK))
    keeps_ref[2] = rate
    chunks = span // CHUNK
    begin = (lax.div(me_ref[0], team) * span).astype(f32)
    times = begin + float(CHUNK) * lax.broadcasted_iota(jnp.int32, (chunks, block), 0).astype(f32)

    @pl.loop(0, modes)
    def _(k):
        ages_ref[k] = jnp.exp(-keeps_ref[2, pl.ds(k, 1), :] * times)


def chunk_rows(group, offset):
    return pl.ds(group * ROWS * CHUNK + offset, ROWS, stride=CHUNK)


def fresh_kernel(team, chosen_ref, table_ref, taps_ref, keeps_ref, conv_ref, carry_ref, fresh, ends):
    seqs, _, _ = chosen_ref.shape
    tiles, span = conv_ref.shape[1:3]
    modes = keeps_ref.shape[1]
    chunks = span // CHUNK
    late = lax.div(lax.axis_index("ctx"), team)
    strips = [(b, t) for t in range(tiles) for b in range(seqs)]

    def look_up(begin):
        for b in range(seqs):
            rows = chosen_ref[b, pl.ds(pl.multiple_of(begin, span), span), :]
            found = jnp.dot(rows, table_ref[...], preferred_element_type=f32)
            for t in range(tiles):
                fresh[b, t] = found[:, t * LANES : (t + 1) * LANES]

    def lanes(t):
        return slice(t * LANES, (t + 1) * LANES)

    def finish_chunks(values, b, t, group):
        for k in range(modes):
            keep = jnp.broadcast_to(keeps_ref[0, k : k + 1, lanes(t)], (ROWS, LANES))
            total = keep * values[0]
            for value in values[1:]:
                total = keep * (total + value)
            ends[b, t, chunk_rows(group, k), :] = total

    def values_of(b, t, group):
        return [fresh[b, t, chunk_rows(group, i), :] for i in range(CHUNK)]

    def rows_of(chunk):
        return pl.ds(pl.multiple_of(chunk * modes, modes), modes)

    for b, t in strips:
        carry_ref[b, t, 0:modes, :] = jnp.zeros((modes, LANES), f32)

    @pl.when(late == 1)
    def _():
        look_up(0)

        @pl.loop(0, chunks // ROWS)
        def _(group):
            for b, t in strips:
                finish_chunks(values_of(b, t, group), b, t, group)

        def advance(chunk, carries):
            return tuple(
                keeps_ref[1, :, lanes(t)] * carry + ends[b, t, rows_of(chunk), :] for (b, t), carry in zip(strips, carries)
            )

        carries = lax.fori_loop(0, chunks, advance, (jnp.zeros((modes, LANES), f32),) * len(strips))
        for (b, t), carry in zip(strips, carries):
            carry_ref[b, t, 0:modes, :] = carry

    look_up(late * span)

    @pl.loop(0, chunks // ROWS)
    def _(group):
        for b, t in strips:
            values = values_of(b, t, group)
            taps = [jnp.broadcast_to(taps_ref[d : d + 1, lanes(t)], (ROWS, LANES)) for d in range(CHUNK)]
            for i in range(CHUNK):
                total = taps[0] * values[i]
                for d in range(1, i + 1):
                    total = total + taps[d] * values[i - d]
                conv_ref[b, t, chunk_rows(group, i), :] = total
            finish_chunks(values, b, t, group)

    @pl.loop(1, chunks)
    def _(chunk):
        for b, t in strips:
            old, new = rows_of(chunk - 1), rows_of(chunk)
            carry_ref[b, t, new, :] = keeps_ref[1, :, lanes(t)] * carry_ref[b, t, old, :] + ends[b, t, old, :]


def mix_kernel(near_ref, far_ref, conv_ref, carry_ref, weights_ref, ages_ref, out_ref, state, total_ref):
    seqs, tiles, span, _ = conv_ref.shape
    modes = near_ref.shape[1]
    chunks = span // CHUNK
    for b in range(seqs):
        state[b] = near_ref[b] + far_ref[b]

    @pl.loop(0, chunks // ROWS)
    def _(group):
        old = pl.ds(pl.multiple_of(group * ROWS, ROWS), ROWS)
        for t in range(tiles):
            at = slice(t * LANES, (t + 1) * LANES)
            begun = [
                [
                    carry_ref[b, t, chunk_rows(group, k), :] + ages_ref[k, old, at] * state[b, k : k + 1, at]
                    for k in range(modes)
                ]
                for b in range(seqs)
            ]
            for i in range(CHUNK):
                weights = [weights_ref[i, k : k + 1, at] for k in range(modes)]
                for b in range(seqs):
                    total = conv_ref[b, t, chunk_rows(group, i), :]
                    other = weights[0] * begun[b][0]
                    for k in range(1, modes):
                        if k % 2:
                            total = total + weights[k] * begun[b][k]
                        else:
                            other = other + weights[k] * begun[b][k]
                    total_ref[b, t, chunk_rows(0, i), :] = total + other
        for chunk in range(ROWS):
            first = pl.multiple_of((group * ROWS + chunk) * CHUNK, CHUNK)
            for b, t in ((b, t) for b in range(seqs) for t in range(tiles)):
                at = slice(t * LANES, (t + 1) * LANES)
                mixed = total_ref[b, t, chunk * CHUNK : (chunk + 1) * CHUNK, :].astype(jnp.bfloat16)
                if len(out_ref.shape) == 4:
                    own = out_ref.shape[2]
                    spot = pl.ds(pl.multiple_of(lax.rem(first, own), CHUNK), CHUNK)
                    out_ref[lax.div(first, own), b, spot, at] = mixed
                else:
                    out_ref[b, pl.ds(first, CHUNK), at] = mixed


def join_kernel(mixed_ref, out_ref, sem):
    count, _, _, block = mixed_ref.shape
    copies = [
        pltpu.make_async_copy(mixed_ref.at[p], out_ref.at[:, :, pl.ds(p * block, block)], sem.at[p])
        for p in range(count)
    ]
    for copy in copies:
        copy.start()
    for copy in copies:
        copy.wait()


def call(kernel, grid, scalars, in_specs, out_specs, out_shape, flops, moved, scratch=()):
    return pl.pallas_call(
        kernel,
        grid_spec=pltpu.PrefetchScalarGridSpec(
            num_scalar_prefetch=scalars,
            grid=grid,
            in_specs=in_specs,
            out_specs=out_specs,
            scratch_shapes=scratch,
        ),
        out_shape=out_shape,
        cost_estimate=pl.CostEstimate(flops=flops, bytes_accessed=moved, transcendentals=0),
        compiler_params=pltpu.CompilerParams(vmem_limit_bytes=VMEM),
    )


def body(history, lengths, token_ids, embed, residue, decay, skip):
    devices = lax.axis_size("ctx")
    me = lax.axis_index("ctx")
    seqs, tile, width = history.shape
    modes = decay.shape[0]
    rows = embed.shape[0]
    gen = token_ids.shape[1]
    total_len = float(tile * devices)
    team = devices // 2
    chips = team // 2
    bits = chips.bit_length() - 1
    assert devices == 4 * 2**bits
    block = width // team
    span = gen // 2
    chunks = span // CHUNK
    tiles = block // LANES
    assert block % LANES == 0 and span % (ROWS * CHUNK) == 0
    own = gen // devices
    place = me.astype(jnp.int32).reshape(1)
    history, embed, residue, decay, skip, lengths = (
        pltpu.with_memory_space_constraint(x, pltpu.HBM)
        for x in (history, embed, residue, decay, skip.reshape(1, width), lengths)
    )
    chip = lax.rem(me, team) // 2
    opposite = [(j, (j + team) % devices) for j in range(devices)]
    shape = jax.ShapeDtypeStruct

    def paired(x, distance):
        return lax.ppermute(x, "ctx", [(j, j ^ distance) for j in range(devices)])

    swapped = pltpu.with_memory_space_constraint(paired(history, 1), pltpu.VMEM)

    hbm = pl.BlockSpec(memory_space=pltpu.HBM)
    vmem = pl.BlockSpec(memory_space=pltpu.VMEM)
    half = chips // 2
    columns, states, decays, held, ends = call(
        lambda *refs: prepare_kernel(total_len, bits, *refs),
        (1,),
        0,
        [hbm] * 4,
        [hbm, vmem, vmem, vmem, vmem],
        [
            shape((devices, rows, block), jnp.bfloat16),
            shape((half, seqs, modes, block), f32),
            shape((chips, modes, block), f32),
            shape((half, seqs, tile, block), jnp.bfloat16),
            shape((seqs, block), jnp.int32),
        ],
        2 * seqs * tile * modes * block * half,
        2**20,
        [
            pltpu.VMEM((team, rows, block), jnp.bfloat16),
            pltpu.VMEM((half, seqs, tile, block), jnp.bfloat16),
            pltpu.VMEM((seqs, tile, block), f32),
            pltpu.SMEM((seqs,), jnp.int32),
            pltpu.SemaphoreType.DMA(()),
            pltpu.SemaphoreType.DMA((team,)),
            pltpu.SemaphoreType.DMA((chips,)),
            pltpu.SemaphoreType.DMA((chips,)),
            pltpu.SemaphoreType.DMA((2,)),
        ],
    )(lengths, embed, history, decay)
    table = lax.all_to_all(columns, "ctx", 0, 0, tiled=True)
    table = table.reshape(devices * rows, block)

    def finish(kernel, operand, flops):
        return call(
            lambda *refs: kernel(total_len, bits, *refs),
            (1,),
            0,
            [vmem] * 4,
            vmem,
            shape((half, seqs, modes, block), f32),
            flops,
            2**20,
            [pltpu.VMEM((seqs, tile, block), f32)],
        )(ends, swapped, operand, decays)

    work = 2 * seqs * tile * modes * block * half
    sent = finish(give_kernel, states, work)
    came = paired(sent, 2**bits)
    mine = finish(keep_kernel, held, 2 * work) + came
    done = 0
    while done < bits - 1:
        now = min(2, bits - 1 - done)
        ways, size = 2**now, mine.shape[0] // 2**now
        digit = lax.rem(lax.div(chip, 2**done), ways)
        take = lambda x, d: lax.dynamic_slice_in_dim(x, reverse_bits(d, now) * size, size, 0)
        total = take(mine, digit)
        for d in range(ways - 1, 0, -1):
            flipped = digit ^ d
            total = total + paired(take(mine, flipped), d << (done + 1))
        mine = total
        done += now
    near = mine[0]
    far = lax.ppermute(near, "ctx", opposite)

    entry = lax.broadcasted_iota(jnp.int32, (seqs, gen, devices * rows), 2)
    chosen = (token_ids[:, :, None] == entry).astype(jnp.bfloat16)
    strip = lambda g, at: (0, lax.rem(at[0], team))
    weights, taps, keeps, ages = call(
        lambda *refs: tables_kernel(total_len, team, span, *refs),
        (1,),
        1,
        [pl.BlockSpec((modes, block), strip)] * 2 + [pl.BlockSpec((1, block), strip)],
        [vmem] * 4,
        [
            shape((CHUNK, modes, block), f32),
            shape((CHUNK, block), f32),
            shape((3, modes, block), f32),
            shape((modes, chunks, block), f32),
        ],
        10**6,
        2**20,
    )(place, decay, residue, skip)
    conv, carry = call(
        lambda *refs: fresh_kernel(team, *refs),
        (1,),
        0,
        [vmem] * 4,
        [vmem] * 2,
        [shape((seqs, tiles, span, LANES), f32), shape((seqs, tiles, chunks * modes, LANES), f32)],
        6 * seqs * span * modes * block,
        2**21,
        [pltpu.VMEM((seqs, tiles, span, LANES), f32), pltpu.VMEM((seqs, tiles, chunks * modes, LANES), f32)],
    )(chosen, table, taps, keeps)

    direct = own % CHUNK == 0
    mixed = call(
        mix_kernel,
        (1,),
        0,
        [vmem] * 6,
        vmem,
        shape((team, seqs, own, block) if direct else (seqs, span, block), jnp.bfloat16),
        3 * seqs * span * modes * block,
        2**21,
        [pltpu.VMEM((seqs, modes, block), f32), pltpu.VMEM((seqs, tiles, ROWS * CHUNK, LANES), f32)],
    )(near, far, conv, carry, weights, ages)
    if not direct:
        mixed = mixed.reshape(seqs, team, own, block).transpose(1, 0, 2, 3)
    halves = [[h * team + p for p in range(team)] for h in range(2)]
    result = lax.all_to_all(mixed, "ctx", 0, 0, tiled=True, axis_index_groups=halves)
    return call(
        join_kernel,
        (1,),
        0,
        [vmem],
        hbm,
        shape((seqs, own, width), jnp.bfloat16),
        10**5,
        2**20,
        [pltpu.SemaphoreType.DMA((team,))],
    )(result)


def solution(mesh):
    placed = (P("group", "ctx", None), P("group"), P("group", None), P("ctx", None), P(), P(), P())
    return jax.shard_map(body, mesh=mesh, in_specs=placed, out_specs=P("group", "ctx", None), check_vma=False)
```

```python
import jax
import jax.numpy as jnp
from jax import lax
from jax.experimental import pallas as pl
from jax.experimental.pallas import tpu as pltpu
from jax.sharding import PartitionSpec as P

ROWS = 8
CHUNK = 16
LANES = 128
VMEM = 16 * 2**20
f32 = jnp.float32


def reverse_bits(value, bits):
    result = 0
    for k in range(bits):
        result = result + lax.rem(lax.div(value, 2**k), 2) * 2 ** (bits - 1 - k)
    return result


def merge_rows(parts):
    row = lax.broadcasted_iota(jnp.int32, parts[0].shape, 0)
    low = row < 4
    level = [
        jnp.where(low, parts[i], parts[i + 4]) + pltpu.roll(jnp.where(low, parts[i + 4], parts[i]), 4, 0)
        for i in range(4)
    ]
    for gap in (2, 1):
        first = (row & gap) == 0
        level = [
            jnp.where(first, level[i], level[i + gap])
            + jnp.where(first, pltpu.roll(level[i], 8 - gap, 0), pltpu.roll(level[i + gap], gap, 0))
            for i in range(gap)
        ]
    return level[0]


def fold(x):
    total = x[:ROWS]
    for start in range(ROWS, x.shape[0], ROWS):
        total = total + x[start : start + ROWS]
    return total


def horner(keep, rows_of, count, tile):
    def step(s, sums):
        return tuple(keep * total + rows_of(i, s) for i, total in enumerate(sums))

    return lax.fori_loop(0, tile, step, (jnp.zeros(keep.shape, f32),) * count, unroll=True)


def block_of(me, spot, give, bits):
    core = lax.rem(me, 2)
    top = lax.rem(lax.div(me, 2**bits), 2)
    if give:
        top = 1 - top
    return 2 * (top * 2 ** (bits - 1) + reverse_bits(spot, bits - 1)) + core


def masked(value, length, start):
    row = lax.broadcasted_iota(jnp.int32, value.shape, 0)
    return jnp.where(row < length - start, value.astype(f32), 0.0)


def lift(rate, length, end, tile):
    return jnp.exp(-rate * (jnp.maximum(length - end, -tile) + 1).astype(f32))


def prepare_kernel(
    total_len, bits, lengths_ref, embed_ref, history_ref, decay_ref,
    columns_ref, states_ref, decays_ref, held_ref, ends_ref,
    entries, pieces, wide, lengths, length_sem, load_sem, piece_sem, rate_sem, store_sem,
):
    count, _, block = columns_ref.shape
    half, seqs, tile, _ = pieces.shape
    team = count // 2
    me = lax.axis_index("ctx")

    def fetch(spot, give):
        start = pl.multiple_of(block_of(me, spot, give, bits) * block, block)
        target, index = (pieces, spot) if give else (held_ref, spot + half)
        return (
            pltpu.make_async_copy(decay_ref.at[:, pl.ds(start, block)], decays_ref.at[index], rate_sem.at[index]),
            pltpu.make_async_copy(history_ref.at[:, :, pl.ds(start, block)], target.at[spot], piece_sem.at[index]),
        )

    copies = [copy for give in (True, False) for spot in range(half) for copy in fetch(spot, give)]
    loads = [
        pltpu.make_async_copy(embed_ref.at[:, pl.ds(p * block, block)], entries.at[p], load_sem.at[p])
        for p in range(team)
    ]
    stores = [
        pltpu.make_async_copy(entries, columns_ref.at[pl.ds(h * team, team)], store_sem.at[h]) for h in range(2)
    ]
    length_copy = pltpu.make_async_copy(lengths_ref, lengths, length_sem)
    for copy in [length_copy] + loads + copies:
        copy.start()
    for copy in loads:
        copy.wait()
    for copy in stores:
        copy.start()
    length_copy.wait()
    for b in range(seqs):
        ends_ref[b : b + 1, :] = jnp.full((1, block), lengths[b], jnp.int32)
    for copy in copies[: 2 * half]:
        copy.wait()

    @pl.loop(0, half)
    def _(spot):
        rate = decays_ref[spot] / total_len
        sums = partial_states(rate, lambda b: pieces[spot, b], wide, ends_ref, me * tile)
        for b in range(seqs):
            states_ref[spot, b] = sums[b]

    for copy in copies[2 * half :] + stores:
        copy.wait()


def partial_states(rate, tile_of, wide, ends_ref, start):
    seqs, tile, _ = wide.shape
    keep = jnp.exp(-rate)
    for b in range(seqs):
        wide[b] = masked(tile_of(b), ends_ref[b : b + 1, :], start)
    sums = horner(keep, lambda b, s: wide[b, pl.ds(s, 1), :], seqs, tile)
    return [sums[b] * lift(rate, ends_ref[b : b + 1, :], start + tile, tile) for b in range(seqs)]


def give_kernel(total_len, bits, ends_ref, other_ref, states_ref, decays_ref, out_ref, wide):
    seqs, tile, block = wide.shape
    me = lax.axis_index("ctx")
    partner = me + 1 - 2 * lax.rem(me, 2)

    @pl.loop(0, out_ref.shape[0])
    def _(spot):
        at = pl.ds(pl.multiple_of(block_of(me, spot, True, bits) * block, block), block)
        rate = decays_ref[spot] / total_len
        sums = partial_states(rate, lambda b: other_ref[b, :, at], wide, ends_ref, partner * tile)
        for b in range(seqs):
            out_ref[spot, b] = states_ref[spot, b] + sums[b]


def keep_kernel(total_len, bits, ends_ref, other_ref, held_ref, decays_ref, out_ref, wide):
    seqs, tile, block = wide.shape
    half = out_ref.shape[0]
    me = lax.axis_index("ctx")
    partner = me + 1 - 2 * lax.rem(me, 2)

    @pl.loop(0, half)
    def _(spot):
        at = pl.ds(pl.multiple_of(block_of(me, spot, False, bits) * block, block), block)
        rate = decays_ref[spot + half] / total_len
        own = partial_states(rate, lambda b: held_ref[spot, b], wide, ends_ref, me * tile)
        sums = partial_states(rate, lambda b: other_ref[b, :, at], wide, ends_ref, partner * tile)
        for b in range(seqs):
            out_ref[spot, b] = own[b] + sums[b]


def tables_kernel(total_len, team, span, me_ref, decay_ref, residue_ref, skip_ref, weights_ref, taps_ref, keeps_ref, ages_ref):
    modes, block = decay_ref.shape
    rate = decay_ref[...] / total_len
    residue = residue_ref[...]
    taps = []
    for i in range(CHUNK):
        weight = residue * jnp.exp(-rate * float(i))
        weights_ref[i] = weight
        taps.append(fold(weight))
    for start in range(0, CHUNK, ROWS):
        taps_ref[start : start + ROWS] = merge_rows(taps[start : start + ROWS])
    taps_ref[0:1] = taps_ref[0:1] + skip_ref[...]
    keeps_ref[0] = jnp.exp(-rate)
    keeps_ref[1] = jnp.exp(-rate * float(CHUNK))
    keeps_ref[2] = rate
    chunks = span // CHUNK
    begin = (lax.div(me_ref[0], team) * span).astype(f32)
    times = begin + float(CHUNK) * lax.broadcasted_iota(jnp.int32, (chunks, block), 0).astype(f32)

    @pl.loop(0, modes)
    def _(k):
        ages_ref[k] = jnp.exp(-keeps_ref[2, pl.ds(k, 1), :] * times)


def chunk_rows(group, offset):
    return pl.ds(group * ROWS * CHUNK + offset, ROWS, stride=CHUNK)


def fresh_kernel(team, chosen_ref, table_ref, taps_ref, keeps_ref, conv_ref, carry_ref, fresh, ends):
    seqs, _, _ = chosen_ref.shape
    tiles, span = conv_ref.shape[1:3]
    modes = keeps_ref.shape[1]
    chunks = span // CHUNK
    late = lax.div(lax.axis_index("ctx"), team)
    strips = [(b, t) for t in range(tiles) for b in range(seqs)]

    def look_up(begin):
        for b in range(seqs):
            rows = chosen_ref[b, pl.ds(pl.multiple_of(begin, span), span), :]
            found = jnp.dot(rows, table_ref[...], preferred_element_type=f32)
            for t in range(tiles):
                fresh[b, t] = found[:, t * LANES : (t + 1) * LANES]

    def lanes(t):
        return slice(t * LANES, (t + 1) * LANES)

    def finish_chunks(values, b, t, group):
        for k in range(modes):
            keep = jnp.broadcast_to(keeps_ref[0, k : k + 1, lanes(t)], (ROWS, LANES))
            total = keep * values[0]
            for value in values[1:]:
                total = keep * (total + value)
            ends[b, t, chunk_rows(group, k), :] = total

    def values_of(b, t, group):
        return [fresh[b, t, chunk_rows(group, i), :] for i in range(CHUNK)]

    def rows_of(chunk):
        return pl.ds(pl.multiple_of(chunk * modes, modes), modes)

    for b, t in strips:
        carry_ref[b, t, 0:modes, :] = jnp.zeros((modes, LANES), f32)

    @pl.when(late == 1)
    def _():
        look_up(0)

        @pl.loop(0, chunks // ROWS)
        def _(group):
            for b, t in strips:
                finish_chunks(values_of(b, t, group), b, t, group)

        def advance(chunk, carries):
            return tuple(
                keeps_ref[1, :, lanes(t)] * carry + ends[b, t, rows_of(chunk), :] for (b, t), carry in zip(strips, carries)
            )

        carries = lax.fori_loop(0, chunks, advance, (jnp.zeros((modes, LANES), f32),) * len(strips), unroll=4)
        for (b, t), carry in zip(strips, carries):
            carry_ref[b, t, 0:modes, :] = carry

    look_up(late * span)

    @pl.loop(0, chunks // ROWS)
    def _(group):
        for b, t in strips:
            values = values_of(b, t, group)
            taps = [jnp.broadcast_to(taps_ref[d : d + 1, lanes(t)], (ROWS, LANES)) for d in range(CHUNK)]
            for i in range(CHUNK):
                total = taps[0] * values[i]
                for d in range(1, i + 1):
                    total = total + taps[d] * values[i - d]
                conv_ref[b, t, chunk_rows(group, i), :] = total
            finish_chunks(values, b, t, group)

    def settle(chunk, carries):
        settled = []
        for (b, t), carry in zip(strips, carries):
            carry = keeps_ref[1, :, lanes(t)] * carry + ends[b, t, rows_of(chunk), :]
            carry_ref[b, t, rows_of(chunk + 1), :] = carry
            settled.append(carry)
        return tuple(settled)

    begun = tuple(carry_ref[b, t, 0:modes, :] for b, t in strips)
    lax.fori_loop(0, chunks - 1, settle, begun, unroll=5)


def mix_kernel(near_ref, far_ref, conv_ref, carry_ref, weights_ref, ages_ref, out_ref, state, total_ref):
    seqs, tiles, span, _ = conv_ref.shape
    modes = near_ref.shape[1]
    chunks = span // CHUNK
    for b in range(seqs):
        state[b] = near_ref[b] + far_ref[b]

    @pl.loop(0, chunks // ROWS)
    def _(group):
        old = pl.ds(pl.multiple_of(group * ROWS, ROWS), ROWS)
        for t in range(tiles):
            at = slice(t * LANES, (t + 1) * LANES)
            begun = [
                [
                    carry_ref[b, t, chunk_rows(group, k), :] + ages_ref[k, old, at] * state[b, k : k + 1, at]
                    for k in range(modes)
                ]
                for b in range(seqs)
            ]
            for i in range(CHUNK):
                weights = [weights_ref[i, k : k + 1, at] for k in range(modes)]
                for b in range(seqs):
                    total = conv_ref[b, t, chunk_rows(group, i), :]
                    other = weights[0] * begun[b][0]
                    for k in range(1, modes):
                        if k % 2:
                            total = total + weights[k] * begun[b][k]
                        else:
                            other = other + weights[k] * begun[b][k]
                    total_ref[b, t, chunk_rows(0, i), :] = total + other
        for chunk in range(ROWS):
            first = pl.multiple_of((group * ROWS + chunk) * CHUNK, CHUNK)
            for b, t in ((b, t) for b in range(seqs) for t in range(tiles)):
                at = slice(t * LANES, (t + 1) * LANES)
                mixed = total_ref[b, t, chunk * CHUNK : (chunk + 1) * CHUNK, :].astype(jnp.bfloat16)
                if len(out_ref.shape) == 4:
                    own = out_ref.shape[2]
                    spot = pl.ds(pl.multiple_of(lax.rem(first, own), CHUNK), CHUNK)
                    out_ref[lax.div(first, own), b, spot, at] = mixed
                else:
                    out_ref[b, pl.ds(first, CHUNK), at] = mixed


def join_kernel(mixed_ref, out_ref, sem):
    count, _, _, block = mixed_ref.shape
    copies = [
        pltpu.make_async_copy(mixed_ref.at[p], out_ref.at[:, :, pl.ds(p * block, block)], sem.at[p])
        for p in range(count)
    ]
    for copy in copies:
        copy.start()
    for copy in copies:
        copy.wait()


def call(kernel, grid, scalars, in_specs, out_specs, out_shape, flops, moved, scratch=()):
    return pl.pallas_call(
        kernel,
        grid_spec=pltpu.PrefetchScalarGridSpec(
            num_scalar_prefetch=scalars,
            grid=grid,
            in_specs=in_specs,
            out_specs=out_specs,
            scratch_shapes=scratch,
        ),
        out_shape=out_shape,
        cost_estimate=pl.CostEstimate(flops=flops, bytes_accessed=moved, transcendentals=0),
        compiler_params=pltpu.CompilerParams(vmem_limit_bytes=VMEM),
    )


def body(history, lengths, token_ids, embed, residue, decay, skip):
    devices = lax.axis_size("ctx")
    me = lax.axis_index("ctx")
    seqs, tile, width = history.shape
    modes = decay.shape[0]
    rows = embed.shape[0]
    gen = token_ids.shape[1]
    total_len = float(tile * devices)
    team = devices // 2
    chips = team // 2
    bits = chips.bit_length() - 1
    assert devices == 4 * 2**bits
    block = width // team
    span = gen // 2
    chunks = span // CHUNK
    tiles = block // LANES
    assert block % LANES == 0 and span % (ROWS * CHUNK) == 0
    own = gen // devices
    place = me.astype(jnp.int32).reshape(1)
    history, embed, residue, decay, skip, lengths = (
        pltpu.with_memory_space_constraint(x, pltpu.HBM)
        for x in (history, embed, residue, decay, skip.reshape(1, width), lengths)
    )
    chip = lax.rem(me, team) // 2
    opposite = [(j, (j + team) % devices) for j in range(devices)]
    shape = jax.ShapeDtypeStruct

    def paired(x, distance):
        return lax.ppermute(x, "ctx", [(j, j ^ distance) for j in range(devices)])

    swapped = pltpu.with_memory_space_constraint(paired(history, 1), pltpu.VMEM)

    hbm = pl.BlockSpec(memory_space=pltpu.HBM)
    vmem = pl.BlockSpec(memory_space=pltpu.VMEM)
    half = chips // 2
    columns, states, decays, held, ends = call(
        lambda *refs: prepare_kernel(total_len, bits, *refs),
        (1,),
        0,
        [hbm] * 4,
        [hbm, vmem, vmem, vmem, vmem],
        [
            shape((devices, rows, block), jnp.bfloat16),
            shape((half, seqs, modes, block), f32),
            shape((chips, modes, block), f32),
            shape((half, seqs, tile, block), jnp.bfloat16),
            shape((seqs, block), jnp.int32),
        ],
        2 * seqs * tile * modes * block * half,
        2**20,
        [
            pltpu.VMEM((team, rows, block), jnp.bfloat16),
            pltpu.VMEM((half, seqs, tile, block), jnp.bfloat16),
            pltpu.VMEM((seqs, tile, block), f32),
            pltpu.SMEM((seqs,), jnp.int32),
            pltpu.SemaphoreType.DMA(()),
            pltpu.SemaphoreType.DMA((team,)),
            pltpu.SemaphoreType.DMA((chips,)),
            pltpu.SemaphoreType.DMA((chips,)),
            pltpu.SemaphoreType.DMA((2,)),
        ],
    )(lengths, embed, history, decay)
    table = lax.all_to_all(columns, "ctx", 0, 0, tiled=True)
    table = table.reshape(devices * rows, block)

    def finish(kernel, operand, flops):
        return call(
            lambda *refs: kernel(total_len, bits, *refs),
            (1,),
            0,
            [vmem] * 4,
            vmem,
            shape((half, seqs, modes, block), f32),
            flops,
            2**20,
            [pltpu.VMEM((seqs, tile, block), f32)],
        )(ends, swapped, operand, decays)

    work = 2 * seqs * tile * modes * block * half
    sent = finish(give_kernel, states, work)
    came = paired(sent, 2**bits)
    mine = finish(keep_kernel, held, 2 * work) + came
    done = 0
    while done < bits - 1:
        now = min(2, bits - 1 - done)
        ways, size = 2**now, mine.shape[0] // 2**now
        digit = lax.rem(lax.div(chip, 2**done), ways)
        take = lambda x, d: lax.dynamic_slice_in_dim(x, reverse_bits(d, now) * size, size, 0)
        total = take(mine, digit)
        for d in range(ways - 1, 0, -1):
            flipped = digit ^ d
            total = total + paired(take(mine, flipped), d << (done + 1))
        mine = total
        done += now
    near = mine[0]
    far = lax.ppermute(near, "ctx", opposite)

    entry = lax.broadcasted_iota(jnp.int32, (seqs, gen, devices * rows), 2)
    chosen = (token_ids[:, :, None] == entry).astype(jnp.bfloat16)
    strip = lambda g, at: (0, lax.rem(at[0], team))
    weights, taps, keeps, ages = call(
        lambda *refs: tables_kernel(total_len, team, span, *refs),
        (1,),
        1,
        [pl.BlockSpec((modes, block), strip)] * 2 + [pl.BlockSpec((1, block), strip)],
        [vmem] * 4,
        [
            shape((CHUNK, modes, block), f32),
            shape((CHUNK, block), f32),
            shape((3, modes, block), f32),
            shape((modes, chunks, block), f32),
        ],
        10**6,
        2**20,
    )(place, decay, residue, skip)
    conv, carry = call(
        lambda *refs: fresh_kernel(team, *refs),
        (1,),
        0,
        [vmem] * 4,
        [vmem] * 2,
        [shape((seqs, tiles, span, LANES), f32), shape((seqs, tiles, chunks * modes, LANES), f32)],
        6 * seqs * span * modes * block,
        2**21,
        [pltpu.VMEM((seqs, tiles, span, LANES), f32), pltpu.VMEM((seqs, tiles, chunks * modes, LANES), f32)],
    )(chosen, table, taps, keeps)

    direct = own % CHUNK == 0
    mixed = call(
        mix_kernel,
        (1,),
        0,
        [vmem] * 6,
        vmem,
        shape((team, seqs, own, block) if direct else (seqs, span, block), jnp.bfloat16),
        3 * seqs * span * modes * block,
        2**21,
        [pltpu.VMEM((seqs, modes, block), f32), pltpu.VMEM((seqs, tiles, ROWS * CHUNK, LANES), f32)],
    )(near, far, conv, carry, weights, ages)
    if not direct:
        mixed = mixed.reshape(seqs, team, own, block).transpose(1, 0, 2, 3)
    halves = [[h * team + p for p in range(team)] for h in range(2)]
    result = lax.all_to_all(mixed, "ctx", 0, 0, tiled=True, axis_index_groups=halves)
    return call(
        join_kernel,
        (1,),
        0,
        [vmem],
        hbm,
        shape((seqs, own, width), jnp.bfloat16),
        10**5,
        2**20,
        [pltpu.SemaphoreType.DMA((team,))],
    )(result)


def solution(mesh):
    placed = (P("group", "ctx", None), P("group"), P("group", None), P("ctx", None), P(), P(), P())
    return jax.shard_map(body, mesh=mesh, in_specs=placed, out_specs=P("group", "ctx", None), check_vma=False)
```
